256 devices in a mesh: chain: 8 (over z), inner: 32 (over y, x, core).
Axes of the slice: x: 4, y: 4, z: 8, core: 2. Of those that a mesh axis runs over, the one named last changes fastest.
Arguments:
- queries: bfloat16 [32768, 4096], P(('chain', 'inner')), may hold values from -0.75 to 0.75
- key_rows: bfloat16 [32768, 4096], P(('chain', 'inner')), may hold values from -0.75 to 0.75
- value_rows: bfloat16 [32768, 4096], P(('chain', 'inner')), may hold values from -0.75 to 0.75
- out_grad: bfloat16 [32768, 4096], P(('chain', 'inner')), may hold values from -0.75 to 0.75
- log_decay: bfloat16 [32768, 32], P(('chain', 'inner')), may hold values from -2 to 0, as said below
Outputs:
- attended: bfloat16 [32768, 4096], P(('chain', 'inner'))
- query_grad: bfloat16 [32768, 4096], P(('chain', 'inner'))
- key_grad: bfloat16 [32768, 4096], P(('chain', 'inner'))
- value_grad: bfloat16 [32768, 4096], P(('chain', 'inner'))
The draws below stay inside these ranges and needn't reach their ends.
Inputs may be any that keep to these rules, and one draw needn't show every extreme that they name: `log_decay`: every entry is negative.
All inputs are finite; a program needn't handle non-finite values.
Results may differ from the reference program's by a relative error of at most 0.0051.
Values may be sent and summed in bfloat16 or wider, within the bound.
No kernel may reach another device: no remote copies, remote signals or barrier semaphores. Data moves between devices by JAX's collectives and lax.ppermute only.
A program may use at most 64 MiB of HBM per device.

```python
import jax
import jax.numpy as jnp
from jax import lax

HEAD_SIZE = 128
HEAD_COUNT = 32
BLOCK = 128
TOKEN_COUNT = 32768


def draw_log_decay(key, part):
    parallel_sequences = jax.random.split(key, 5)
    quick_heads = jax.random.randint(parallel_sequences[0], (HEAD_COUNT,), 0, 2) == 1
    spread = jnp.exp(jax.random.uniform(parallel_sequences[1], (HEAD_COUNT,), minval=-0.69, maxval=0.69))
    head_decay_speeds = jnp.where(quick_heads, 3.0 / BLOCK, 0.15 / TOKEN_COUNT) * spread
    decay_jitter = jax.random.uniform(parallel_sequences[2], (TOKEN_COUNT, HEAD_COUNT), minval=0.5, maxval=2.0)
    spike_token_rows = jax.random.randint(parallel_sequences[3], (3,), 0, TOKEN_COUNT)
    spike_length = jnp.log(jax.random.uniform(parallel_sequences[4], (3, HEAD_COUNT), minval=0.55, maxval=0.8))
    spike_positions = (jnp.arange(TOKEN_COUNT)[:, None] == spike_token_rows[None, :]).astype(jnp.float32)
    value_inputs = -(head_decay_speeds[None, :] * decay_jitter) + jnp.dot(spike_positions, spike_length)
    return value_inputs.astype(jnp.bfloat16)


def levels(own_key, dims, cuts, least, high):
    level, own = 1.0, jax.random.fold_in(own_key, 6)
    for axis_at, blocks in cuts:
        draws = jnp.exp(jax.random.uniform(jax.random.fold_in(own, axis_at), (blocks,), jnp.float32, least / len(cuts), high / len(cuts)))
        level = level * jnp.repeat(draws, dims[axis_at] // blocks).reshape([-1 if axis == axis_at else 1 for axis in range(len(dims))])
    return level


def bell_draw(rng, dims, width, limit, pieces=(), held_as=jnp.bfloat16):
    drawn = jax.random.normal(rng, dims, jnp.float32) * width
    if len(pieces) > 0:
        drawn = levels(rng, dims, pieces, -0.22, 0.18) * drawn
    return jnp.clip(drawn, min=-limit, max=limit).astype(held_as)


def setup_inputs(seed: int = 0) -> dict:
    key_of = jax.random.split(jax.random.key(seed), 6)
    return {
        "queries": bell_draw(key_of[0], (TOKEN_COUNT, HEAD_COUNT * HEAD_SIZE), 0.125, 0.75, ((0, 256),)),
        "key_rows": bell_draw(key_of[1], (TOKEN_COUNT, HEAD_COUNT * HEAD_SIZE), 0.125, 0.75, ((0, 256),)),
        "value_rows": bell_draw(key_of[2], (TOKEN_COUNT, HEAD_COUNT * HEAD_SIZE), 0.125, 0.75, ((0, 256),)),
        "out_grad": bell_draw(key_of[3], (TOKEN_COUNT, HEAD_COUNT * HEAD_SIZE), 0.125, 0.75, ((0, 256),)),
        "log_decay": draw_log_decay(jax.random.fold_in(key_of[5], 71), 0),
    }


def advance(state, inputs):
    factor, term = inputs
    return jnp.exp(factor) * state + term, state


def narrowed(array):
    return lax.optimization_barrier(array.astype(jnp.bfloat16)).astype(jnp.float32)


def one_head(query_head, key_head, value_head, grad_head, decay_head):
    blocks = TOKEN_COUNT // BLOCK
    highest = lax.Precision.HIGHEST
    query_f = query_head.astype(jnp.float32).reshape(blocks, BLOCK, HEAD_SIZE)
    key_f = key_head.astype(jnp.float32).reshape(blocks, BLOCK, HEAD_SIZE)
    value_f = value_head.astype(jnp.float32).reshape(blocks, BLOCK, HEAD_SIZE)
    grad_f = grad_head.astype(jnp.float32).reshape(blocks, BLOCK, HEAD_SIZE)
    cumul = jnp.cumsum(decay_head.astype(jnp.float32).reshape(blocks, BLOCK), axis=1)
    finals = cumul[:, -1]
    forward_scale = jnp.exp(cumul)[:, :, None]
    backward_scale = jnp.exp(finals[:, None] - cumul)[:, :, None]
    scaled_keys = narrowed(key_f * backward_scale)
    scaled_queries = narrowed(query_f * forward_scale)
    kv_terms = jnp.einsum("jsd,jse->jde", scaled_keys, value_f, precision=highest)
    qd_terms = jnp.einsum("jtd,jte->jde", scaled_queries, grad_f, precision=highest)
    zero_state = jnp.zeros((HEAD_SIZE, HEAD_SIZE), jnp.float32)
    _, entering = lax.scan(advance, zero_state, (finals, kv_terms))
    _, trailing = lax.scan(advance, zero_state, (finals, qd_terms), reverse=True)
    enter_narrow = narrowed(entering)
    trail_narrow = narrowed(trailing)
    positions = jnp.arange(BLOCK)
    lower = positions[:, None] >= positions[None, :]
    weights = jnp.exp(jnp.where(lower[None], cumul[:, :, None] - cumul[:, None, :], -jnp.inf))
    scores = jnp.einsum("jtd,jsd->jts", query_f, key_f, precision=highest)
    probs = narrowed(scores * weights)
    grows = narrowed(jnp.einsum("jte,jse->jts", grad_f, value_f, precision=highest) * weights)
    attended = jnp.einsum("jts,jse->jte", probs, value_f, precision=highest) + forward_scale * jnp.einsum("jtd,jde->jte", query_f, enter_narrow, precision=highest)
    query_grad = jnp.einsum("jts,jsd->jtd", grows, key_f, precision=highest) + forward_scale * jnp.einsum("jte,jde->jtd", grad_f, enter_narrow, precision=highest)
    key_grad = jnp.einsum("jts,jtd->jsd", grows, query_f, precision=highest) + backward_scale * jnp.einsum("jse,jde->jsd", value_f, trail_narrow, precision=highest)
    value_grad = jnp.einsum("jts,jte->jse", probs, grad_f, precision=highest) + backward_scale * jnp.einsum("jsd,jde->jse", key_f, trail_narrow, precision=highest)
    return tuple(item.reshape(TOKEN_COUNT, HEAD_SIZE).astype(jnp.bfloat16) for item in (attended, query_grad, key_grad, value_grad))


def head_major(array):
    return array.reshape(TOKEN_COUNT, HEAD_COUNT, HEAD_SIZE).transpose(1, 0, 2)


def token_major(array):
    return array.transpose(1, 0, 2).reshape(TOKEN_COUNT, HEAD_COUNT * HEAD_SIZE)


def reference(queries, key_rows, value_rows, out_grad, log_decay):
    stacked = (head_major(queries), head_major(key_rows), head_major(value_rows), head_major(out_grad), log_decay.T)
    results = lax.map(lambda items: one_head(items[0], items[1], items[2], items[3], items[4]), stacked)
    return (token_major(results[0]), token_major(results[1]), token_major(results[2]), token_major(results[3]))
```

```python
import jax
import jax.numpy as jnp
from jax import lax
from jax.experimental import pallas as pl
from jax.experimental.pallas import tpu as pltpu
from jax.sharding import Mesh, PartitionSpec as P

HEAD = 128
BLOCK = 128
HALF_HEADS = 16
STEPS = 4
PER_STEP = HALF_HEADS // STEPS
PART = HEAD // 2
TAIL = 16
AXES = ("zh", "zl", "y", "x", "core")
GROUP = ("zl", "y", "x")

F32 = jnp.float32
BF16 = jnp.bfloat16
VMEM_LIMIT = 48 * 1024 * 1024


def dot(left, right, left_dim, right_dim):
    return lax.dot_general(
        left, right, (((left_dim,), (right_dim,)), ((), ())), preferred_element_type=F32
    )


def pack_decay(value):
    full = jnp.broadcast_to(value, (TAIL, HEAD))
    high = full.astype(BF16)
    rest = full - high.astype(F32)
    middle = rest.astype(BF16)
    low = (rest - middle.astype(F32)).astype(BF16)
    row = lax.broadcasted_iota(jnp.int32, (TAIL, HEAD), 0)
    chosen = jnp.where(
        row == 0, high.astype(F32), jnp.where(row == 1, middle.astype(F32), low.astype(F32))
    )
    return chosen.astype(BF16)


def unpack_decay(tile):
    rows = tile.astype(F32)
    return rows[0:1] + rows[1:2] + rows[2:3]


def lower_triangle():
    at = lax.broadcasted_iota(jnp.int32, (BLOCK, BLOCK), 0)
    before = lax.broadcasted_iota(jnp.int32, (BLOCK, BLOCK), 1)
    return at >= before


def half_decay(decay_ref, half):
    decay = decay_ref[...].astype(F32)
    return jnp.where(half == 0, decay[:, :HALF_HEADS], decay[:, HALF_HEADS:]).astype(BF16)


def set_scales(decay_ref, half, fwd_ref, bwd_ref, final_ref, cols_ref=None, rows_ref=None):
    decay = half_decay(decay_ref, half)
    triangle = lower_triangle().astype(F32).astype(BF16)
    cumul = dot(triangle, decay, 1, 0)
    finals = cumul[BLOCK - 1 : BLOCK, :]
    fwd = jnp.exp(cumul)
    bwd = jnp.exp(finals - cumul)
    for step in range(STEPS):
        heads = slice(step * PER_STEP, (step + 1) * PER_STEP)
        fwd_ref[step] = fwd[:, heads]
        bwd_ref[step] = bwd[:, heads]
        final_ref[step] = jnp.broadcast_to(finals[:, heads], (8, PER_STEP))
        if cols_ref is not None:
            cols_ref[step] = cumul[:, heads]
    if rows_ref is not None:
        rows = dot(decay, triangle, 0, 1)
        for step in range(STEPS):
            rows_ref[step] = rows[step * PER_STEP : (step + 1) * PER_STEP]


def head_states(query, key, value, grad, fwd, bwd):
    scaled_key = (key.astype(F32) * bwd).astype(BF16)
    scaled_query = (query.astype(F32) * fwd).astype(BF16)
    return dot(scaled_key, value, 0, 0), dot(scaled_query, grad, 0, 0)


def send_states(
    half_ref, decay_ref, query_ref, key_ref, value_ref, grad_ref, out_ref, fwd_ref, bwd_ref, final_ref
):
    step = pl.program_id(0)

    @pl.when(step == 0)
    def _():
        set_scales(decay_ref, half_ref[0], fwd_ref, bwd_ref, final_ref)

    fwd = fwd_ref[step]
    bwd = bwd_ref[step]
    finals = final_ref[step]
    for head in range(PER_STEP):
        cols = slice(head * HEAD, (head + 1) * HEAD)
        one = slice(head, head + 1)
        kv, qd = head_states(
            query_ref[:, cols], key_ref[:, cols], value_ref[:, cols], grad_ref[:, cols],
            fwd[:, one], bwd[:, one],
        )
        out_ref[head, 0:HEAD, :] = kv.astype(BF16)
        out_ref[head, HEAD : 2 * HEAD, :] = qd.astype(BF16)
        out_ref[head, 2 * HEAD :, :] = pack_decay(finals[0:1, one])


def keep_states(
    half_ref, decay_ref, query_ref, key_ref, value_ref, grad_ref, other_ref,
    own_ref, pair_ref, fwd_ref, bwd_ref, final_ref,
):
    step = pl.program_id(0)
    first = half_ref[0] == 0

    @pl.when(step == 0)
    def _():
        set_scales(decay_ref, half_ref[0], fwd_ref, bwd_ref, final_ref)

    fwd = fwd_ref[step]
    bwd = bwd_ref[step]
    finals = final_ref[step]
    for head in range(PER_STEP):
        cols = slice(head * HEAD, (head + 1) * HEAD)
        one = slice(head, head + 1)
        kv, qd = head_states(
            query_ref[:, cols], key_ref[:, cols], value_ref[:, cols], grad_ref[:, cols],
            fwd[:, one], bwd[:, one],
        )
        mine = jnp.broadcast_to(finals[0:1, one], (1, HEAD))
        theirs = unpack_decay(other_ref[head, 2 * HEAD :, :])
        own_ref[head, 0:HEAD, :] = kv.astype(BF16)
        own_ref[head, HEAD : 2 * HEAD, :] = qd.astype(BF16)
        own_ref[head, 2 * HEAD :, :] = pack_decay(finals[0:1, one])
        other_kv = other_ref[head, 0:HEAD, :].astype(F32)
        other_qd = other_ref[head, HEAD : 2 * HEAD, :].astype(F32)
        decay_mine = jnp.exp(mine)
        decay_theirs = jnp.exp(theirs)
        unit = jnp.ones_like(mine)
        pair_kv = jnp.where(first, decay_theirs, unit) * kv + jnp.where(first, unit, decay_mine) * other_kv
        pair_qd = jnp.where(first, unit, decay_theirs) * qd + jnp.where(first, decay_mine, unit) * other_qd
        pair_kv = pair_kv.astype(BF16)
        pair_qd = pair_qd.astype(BF16)
        tail = pack_decay(mine + theirs)
        for part in range(2):
            rows = slice(part * PART, (part + 1) * PART)
            pair_ref[2 * head + part, 0:PART, :] = pair_kv[rows]
            pair_ref[2 * head + part, PART : 2 * PART, :] = pair_qd[rows]
            pair_ref[2 * head + part, 2 * PART :, :] = tail


def group_total(pieces_ref, out_ref):
    count = pieces_ref.shape[0]
    zero = jnp.zeros((PART, HEAD), F32)

    def hop(at, carry):
        state, trail, total = carry
        back = count - 1 - at
        decay = unpack_decay(pieces_ref[at, 2 * PART :, :])
        decay_back = unpack_decay(pieces_ref[back, 2 * PART :, :])
        state = jnp.exp(decay) * state + pieces_ref[at, 0:PART, :].astype(F32)
        trail = jnp.exp(decay_back) * trail + pieces_ref[back, PART : 2 * PART, :].astype(F32)
        return state, trail, total + decay

    state, trail, total = lax.fori_loop(
        0, count, hop, (zero, zero, jnp.zeros((1, HEAD), F32)), unroll=4
    )
    out_ref[0:PART, :] = state.astype(BF16)
    out_ref[PART : 2 * PART, :] = trail.astype(BF16)
    out_ref[2 * PART :, :] = pack_decay(total)


def group_entries(index_ref, pieces_ref, one_ref, two_ref, three_ref, out_ref):
    count = pieces_ref.shape[0]
    place = index_ref[0]
    state = jnp.zeros((PART, HEAD), F32)
    trail = jnp.zeros((PART, HEAD), F32)
    for distance, ref in ((3, three_ref), (2, two_ref), (1, one_ref)):
        longer = jnp.exp(unpack_decay(ref[2 * PART :, :])) * state + ref[0:PART, :].astype(F32)
        state = jnp.where(place >= distance, longer, state)
    for distance, ref in ((1, one_ref), (2, two_ref), (3, three_ref)):
        longer = jnp.exp(unpack_decay(ref[2 * PART :, :])) * trail + ref[PART : 2 * PART, :].astype(F32)
        trail = jnp.where(place < distance, longer, trail)

    def hop(at, carry):
        state, trail = carry
        back = count - 1 - at
        out_ref[at, 0:PART, :] = state.astype(BF16)
        out_ref[back, PART : 2 * PART, :] = trail.astype(BF16)
        decay = unpack_decay(pieces_ref[at, 2 * PART :, :])
        decay_back = unpack_decay(pieces_ref[back, 2 * PART :, :])
        state = jnp.exp(decay) * state + pieces_ref[at, 0:PART, :].astype(F32)
        trail = jnp.exp(decay_back) * trail + pieces_ref[back, PART : 2 * PART, :].astype(F32)
        return state, trail

    lax.fori_loop(0, count, hop, (state, trail), unroll=4)


def other_entries(half_ref, own_ref, pair_ref, out_ref):
    first = half_ref[0] == 0
    for head in range(PER_STEP):
        decay = jnp.exp(unpack_decay(own_ref[head, 2 * HEAD :, :]))
        for part in range(2):
            rows = slice(part * PART, (part + 1) * PART)
            qd_rows = slice(HEAD + part * PART, HEAD + (part + 1) * PART)
            state = pair_ref[2 * head + part, 0:PART, :].astype(F32)
            trail = pair_ref[2 * head + part, PART : 2 * PART, :].astype(F32)
            later = decay * state + own_ref[head, rows, :].astype(F32)
            earlier = decay * trail + own_ref[head, qd_rows, :].astype(F32)
            out_ref[head, rows, :] = jnp.where(first, later, state).astype(BF16)
            out_ref[head, qd_rows, :] = jnp.where(first, trail, earlier).astype(BF16)


def head_results(query, key, value, grad, col, row, fwd, bwd, entering, trailing, lower):
    weights = jnp.exp(jnp.where(lower, col - row, -jnp.inf))
    probs = (dot(query, key, 1, 1) * weights).astype(BF16)
    grows = (dot(grad, value, 1, 1) * weights).astype(BF16)
    attended = dot(probs, value, 1, 0) + fwd * dot(query, entering, 1, 0)
    query_grad = dot(grows, key, 1, 0) + fwd * dot(grad, entering, 1, 1)
    key_grad = dot(grows, query, 0, 0) + bwd * dot(value, trailing, 1, 1)
    value_grad = dot(probs, grad, 0, 0) + bwd * dot(key, trailing, 1, 0)
    return attended, query_grad, key_grad, value_grad


def own_results(
    half_ref, decay_ref, query_ref, key_ref, value_ref, grad_ref, pair_ref, other_ref,
    att_ref, qg_ref, kg_ref, vg_ref, fwd_ref, bwd_ref, final_ref, cols_ref, rows_ref,
):
    step = pl.program_id(0)
    first = half_ref[0] == 0

    @pl.when(step == 0)
    def _():
        set_scales(decay_ref, half_ref[0], fwd_ref, bwd_ref, final_ref, cols_ref, rows_ref)

    lower = lower_triangle()
    for head in range(PER_STEP):
        cols = slice(head * HEAD, (head + 1) * HEAD)
        one = slice(head, head + 1)
        decay = jnp.exp(unpack_decay(other_ref[head, 2 * HEAD :, :]))
        state = jnp.concatenate(
            [pair_ref[2 * head, 0:PART, :], pair_ref[2 * head + 1, 0:PART, :]], axis=0
        ).astype(F32)
        trail = jnp.concatenate(
            [pair_ref[2 * head, PART : 2 * PART, :], pair_ref[2 * head + 1, PART : 2 * PART, :]], axis=0
        ).astype(F32)
        later = decay * state + other_ref[head, 0:HEAD, :].astype(F32)
        earlier = decay * trail + other_ref[head, HEAD : 2 * HEAD, :].astype(F32)
        results = head_results(
            query_ref[:, cols], key_ref[:, cols], value_ref[:, cols], grad_ref[:, cols],
            cols_ref[step][:, one], rows_ref[step][one], fwd_ref[step][:, one], bwd_ref[step][:, one],
            jnp.where(first, state, later).astype(BF16), jnp.where(first, earlier, trail).astype(BF16),
            lower,
        )
        for ref, item in zip((att_ref, qg_ref, kg_ref, vg_ref), results):
            ref[:, cols] = item.astype(BF16)


def other_results(
    half_ref, decay_ref, query_ref, key_ref, value_ref, grad_ref, entry_ref, a_ref, b_ref, c_ref, d_ref,
    att_ref, qg_ref, kg_ref, vg_ref, fwd_ref, bwd_ref, final_ref, cols_ref, rows_ref,
):
    step = pl.program_id(0)

    @pl.when(step == 0)
    def _():
        set_scales(decay_ref, half_ref[0], fwd_ref, bwd_ref, final_ref, cols_ref, rows_ref)

    lower = lower_triangle()
    for head in range(PER_STEP):
        cols = slice(head * HEAD, (head + 1) * HEAD)
        one = slice(head, head + 1)
        results = head_results(
            query_ref[:, cols], key_ref[:, cols], value_ref[:, cols], grad_ref[:, cols],
            cols_ref[step][:, one], rows_ref[step][one], fwd_ref[step][:, one], bwd_ref[step][:, one],
            entry_ref[head, 0:HEAD, :], entry_ref[head, HEAD : 2 * HEAD, :], lower,
        )
        for ref, item in zip((att_ref, qg_ref, kg_ref, vg_ref), results):
            ref[:, cols] = item.astype(BF16)


def whole(shape):
    return pl.BlockSpec(shape, lambda *_: (0,) * len(shape))


def heads_of_half():
    return pl.BlockSpec((BLOCK, PER_STEP * HEAD), lambda step, half: (0, half[0] * STEPS + step))


def by_step(*shape):
    return pl.BlockSpec(shape, lambda step, half: (step,) + (0,) * (len(shape) - 1))


SCALES = (
    pltpu.VMEM((STEPS, BLOCK, PER_STEP), F32),
    pltpu.VMEM((STEPS, BLOCK, PER_STEP), F32),
    pltpu.VMEM((STEPS, 8, PER_STEP), F32),
)
CUMULS = (
    pltpu.VMEM((STEPS, BLOCK, PER_STEP), F32),
    pltpu.VMEM((STEPS, PER_STEP, BLOCK), F32),
)


def call(kernel, half, operands, in_specs, out_specs, out_shape, scratch=(), grid=(STEPS,), aliases=None):
    return pl.pallas_call(
        kernel,
        out_shape=out_shape,
        grid_spec=pltpu.PrefetchScalarGridSpec(
            num_scalar_prefetch=1, grid=grid, in_specs=in_specs, out_specs=out_specs,
            scratch_shapes=list(scratch),
        ),
        input_output_aliases=aliases or {},
        compiler_params=pltpu.CompilerParams(vmem_limit_bytes=VMEM_LIMIT),
    )(half, *operands)


def shards(queries, key_rows, value_rows, out_grad, log_decay):
    core = lax.axis_index("core")
    mine = core.reshape(1).astype(jnp.int32)
    theirs = 1 - mine
    place = lax.axis_index("zh").reshape(1).astype(jnp.int32)
    rows = (queries, key_rows, value_rows, out_grad)
    row_specs = [whole((BLOCK, 2 * HALF_HEADS))] + [heads_of_half() for _ in rows]
    state_rows = 2 * HEAD + TAIL
    piece_rows = 2 * PART + TAIL
    swap = [(0, 1), (1, 0)]

    sent = call(
        send_states, theirs, (log_decay,) + rows, row_specs, by_step(PER_STEP, state_rows, HEAD),
        jax.ShapeDtypeStruct((HALF_HEADS, state_rows, HEAD), BF16), SCALES,
    )
    other = lax.ppermute(sent, "core", swap)
    own, pairs = call(
        keep_states, mine, (log_decay,) + rows + (other,),
        row_specs + [by_step(PER_STEP, state_rows, HEAD)],
        [by_step(PER_STEP, state_rows, HEAD), by_step(2 * PER_STEP, piece_rows, HEAD)],
        [
            jax.ShapeDtypeStruct((HALF_HEADS, state_rows, HEAD), BF16),
            jax.ShapeDtypeStruct((2 * HALF_HEADS, piece_rows, HEAD), BF16),
        ],
        SCALES,
    )
    pieces = lax.all_to_all(pairs, GROUP, split_axis=0, concat_axis=0, tiled=True)
    total = pl.pallas_call(
        group_total,
        out_shape=jax.ShapeDtypeStruct((piece_rows, HEAD), BF16),
        compiler_params=pltpu.CompilerParams(vmem_limit_bytes=VMEM_LIMIT),
    )(pieces)
    size = lax.axis_size("zh")
    moved = [
        lax.ppermute(total, "zh", [(at, (at + distance) % size) for at in range(size)])
        for distance in (1, 2, 3)
    ]
    entries = call(
        group_entries, place, (pieces, *moved),
        [whole((2 * HALF_HEADS, piece_rows, HEAD))] + [whole((piece_rows, HEAD))] * 3,
        whole((2 * HALF_HEADS, 2 * PART, HEAD)),
        jax.ShapeDtypeStruct((2 * HALF_HEADS, 2 * PART, HEAD), BF16), grid=(1,),
    )
    pair_entries = lax.all_to_all(entries, GROUP, split_axis=0, concat_axis=0, tiled=True)
    leaving = call(
        other_entries, mine, (own, pair_entries),
        [by_step(PER_STEP, state_rows, HEAD), by_step(2 * PER_STEP, 2 * PART, HEAD)],
        by_step(PER_STEP, 2 * HEAD, HEAD),
        jax.ShapeDtypeStruct((HALF_HEADS, 2 * HEAD, HEAD), BF16),
    )
    arrived = lax.ppermute(leaving, "core", swap)
    shapes = [jax.ShapeDtypeStruct(queries.shape, BF16)] * 4
    results = call(
        own_results, mine, (log_decay,) + rows + (pair_entries, other),
        row_specs + [by_step(2 * PER_STEP, 2 * PART, HEAD), by_step(PER_STEP, state_rows, HEAD)],
        [heads_of_half()] * 4, shapes, SCALES + CUMULS,
    )
    results = call(
        other_results, theirs, (log_decay,) + rows + (arrived,) + tuple(results),
        row_specs + [by_step(PER_STEP, 2 * HEAD, HEAD)] + [pl.BlockSpec(memory_space=pl.ANY)] * 4,
        [heads_of_half()] * 4, shapes, SCALES + CUMULS, aliases={7: 0, 8: 1, 9: 2, 10: 3},
    )
    return tuple(results)


def solution(mesh):
    chain, inner = mesh.devices.shape
    grid = Mesh(mesh.devices.reshape(chain // 2, 2, 4, 4, inner // 16), AXES)
    spec = P(AXES, None)
    return jax.shard_map(
        shards, mesh=grid, in_specs=(spec,) * 5, out_specs=(spec,) * 4, check_vma=False
    )
```

```python
import jax
import jax.numpy as jnp
from jax import lax
from jax.experimental import pallas as pl
from jax.experimental.pallas import tpu as pltpu
from jax.sharding import Mesh, PartitionSpec as P

HEAD = 128
BLOCK = 128
HALF_HEADS = 16
STEPS = 4
PER_STEP = HALF_HEADS // STEPS
PART = HEAD // 2
TAIL = 8
SLAB = PER_STEP * HEAD
WIDTH = HALF_HEADS * HEAD
LOADS = 2
LOAD = WIDTH // LOADS
AXES = ("zh", "zl", "y", "x", "core")
GROUP = ("zl", "y", "x")

F32 = jnp.float32
BF16 = jnp.bfloat16
VMEM_LIMIT = 16 * 1024 * 1024


def dot(left, right, left_dim, right_dim):
    return lax.dot_general(
        left, right, (((left_dim,), (right_dim,)), ((), ())), preferred_element_type=F32
    )


def pack_decay(value):
    full = jnp.broadcast_to(value, (TAIL, HEAD))
    high = full.astype(BF16)
    rest = full - high.astype(F32)
    middle = rest.astype(BF16)
    low = (rest - middle.astype(F32)).astype(BF16)
    row = lax.broadcasted_iota(jnp.int32, (TAIL, HEAD), 0)
    chosen = jnp.where(
        row == 0, high.astype(F32), jnp.where(row == 1, middle.astype(F32), low.astype(F32))
    )
    return chosen.astype(BF16)


def unpack_decay(tile):
    rows = tile.astype(F32)
    return rows[0:1] + rows[1:2] + rows[2:3]


def lower_triangle():
    at = lax.broadcasted_iota(jnp.int32, (BLOCK, BLOCK), 0)
    before = lax.broadcasted_iota(jnp.int32, (BLOCK, BLOCK), 1)
    return at >= before


def half_decay(decay_ref, half):
    decay = decay_ref[...].astype(F32)
    return jnp.where(half == 0, decay[:HALF_HEADS], decay[HALF_HEADS:]).astype(BF16)


def column_scales(decay):
    cumul = dot(lower_triangle().astype(F32).astype(BF16), decay, 1, 1)
    finals = cumul[BLOCK - 1 : BLOCK, :]
    return jnp.exp(cumul), jnp.exp(finals - cumul), finals


def set_cumuls(decay, cols_ref, rows_ref):
    triangle = lower_triangle().astype(F32).astype(BF16)
    cumul = dot(triangle, decay, 1, 1)
    rows = dot(decay, triangle, 1, 1)
    for step in range(2 * STEPS):
        heads = slice(step * PER_STEP, (step + 1) * PER_STEP)
        cols_ref[step] = cumul[:, heads]
        rows_ref[step] = rows[heads]


def head_states(query, key, value, grad, fwd, bwd):
    scaled_key = (key.astype(F32) * bwd).astype(BF16)
    scaled_query = (query.astype(F32) * fwd).astype(BF16)
    return dot(scaled_key, value, 0, 0), dot(scaled_query, grad, 0, 0)


def write_states(spot, rows, fwd, bwd, finals, outs):
    cols = slice(spot * HEAD, (spot + 1) * HEAD)
    one = slice(spot, spot + 1)
    query, key, value, grad = (ref[:, cols] for ref in rows)
    kv, qd = head_states(query, key, value, grad, fwd[:, one], bwd[:, one])
    tail = pack_decay(finals[:, one])
    for out_ref in outs:
        out_ref[spot, 0:HEAD, :] = kv.astype(out_ref.dtype)
        out_ref[spot, HEAD : 2 * HEAD, :] = qd.astype(out_ref.dtype)
        out_ref[spot, 2 * HEAD :, :] = tail.astype(out_ref.dtype)


def sent_states(half_ref, decay_hbm, *refs):
    sources, out_ref, away, rows = refs[:4], refs[4], refs[5:9], refs[9:13]
    decay_ref, sems, away_sems, decay_sem = refs[13:]
    half = half_ref[0]

    def fetch(array, at):
        source = pl.multiple_of(half * WIDTH + at * LOAD, LOAD)
        return pltpu.make_async_copy(
            sources[array].at[:, pl.ds(source, LOAD)],
            rows[array].at[:, at * LOAD : (at + 1) * LOAD],
            sems.at[array, at],
        )

    def fetch_away(array):
        source = pl.multiple_of((1 - half) * WIDTH, WIDTH)
        return pltpu.make_async_copy(
            sources[array].at[:, pl.ds(source, WIDTH)], away[array], away_sems.at[array]
        )

    decay_copy = pltpu.make_async_copy(decay_hbm, decay_ref, decay_sem.at[0])
    decay_copy.start()
    for at in range(LOADS):
        for array in range(4):
            fetch(array, at).start()
    for array in range(4):
        fetch_away(array).start()
    decay_copy.wait()
    fwd, bwd, finals = column_scales(half_decay(decay_ref, half))
    for spot in range(HALF_HEADS):
        if spot % (HALF_HEADS // LOADS) == 0:
            for array in range(4):
                fetch(array, spot // (HALF_HEADS // LOADS)).wait()
        write_states(spot, rows, fwd, bwd, finals, (out_ref,))
    for array in range(4):
        fetch_away(array).wait()


def kept_states(half_ref, decay_ref, *refs):
    rows, outs = refs[:4], refs[4:]
    fwd, bwd, finals = column_scales(half_decay(decay_ref, half_ref[0]))
    for spot in range(HALF_HEADS):
        write_states(spot, rows, fwd, bwd, finals, outs)


def pair_states(half_ref, own_ref, other_ref, out_hbm, pair_ref, sems):
    first = half_ref[0] == 0
    chunk = 2 * HALF_HEADS // STEPS

    def send(step):
        spots = slice(step * chunk, (step + 1) * chunk)
        return pltpu.make_async_copy(pair_ref.at[spots], out_hbm.at[spots], sems.at[step])

    for head in range(HALF_HEADS):
        mine = unpack_decay(own_ref[head, 2 * HEAD :, :])
        theirs = unpack_decay(other_ref[head, 2 * HEAD :, :])
        decay_mine = jnp.exp(mine)
        decay_theirs = jnp.exp(theirs)
        unit = jnp.ones_like(mine)
        kv_scales = (jnp.where(first, decay_theirs, unit), jnp.where(first, unit, decay_mine))
        qd_scales = (jnp.where(first, unit, decay_theirs), jnp.where(first, decay_mine, unit))
        tail = pack_decay(mine + theirs)
        for part in range(2):
            piece = 2 * head + part
            for at, (scale_own, scale_other) in ((0, kv_scales), (1, qd_scales)):
                rows = slice(at * HEAD + part * PART, at * HEAD + (part + 1) * PART)
                joined = scale_own * own_ref[head, rows, :] + scale_other * other_ref[
                    head, rows, :
                ].astype(F32)
                pair_ref[piece, at * PART : (at + 1) * PART, :] = joined.astype(BF16)
            pair_ref[piece, 2 * PART :, :] = tail
        if (head + 1) % PER_STEP == 0:
            send(head // PER_STEP).start()
    for step in range(STEPS):
        send(step).wait()


def group_total(index_ref, pieces_ref, *outs):
    count = pieces_ref.shape[0]
    place = index_ref[0]
    zero = jnp.zeros((PART, HEAD), F32)

    def hop(at, carry):
        state, trail, total = carry
        back = count - 1 - at
        decay = unpack_decay(pieces_ref[at, 2 * PART :, :])
        decay_back = unpack_decay(pieces_ref[back, 2 * PART :, :])
        state = jnp.exp(decay) * state + pieces_ref[at, 0:PART, :].astype(F32)
        trail = jnp.exp(decay_back) * trail + pieces_ref[back, PART : 2 * PART, :].astype(F32)
        return state, trail, total + decay

    state, trail, total = lax.fori_loop(
        0, count, hop, (zero, zero, jnp.zeros((1, HEAD), F32)), unroll=8
    )
    tail = jnp.broadcast_to(total, (TAIL, HEAD))
    for distance, ref in enumerate(outs, 1):
        ref[0:PART, :] = jnp.where(place + distance <= len(outs), state, trail)
        ref[PART:, :] = tail


def group_entries(index_ref, pieces_ref, one_ref, two_ref, three_ref, out_ref):
    count = pieces_ref.shape[0]
    place = index_ref[0]
    state = jnp.zeros((PART, HEAD), F32)
    trail = jnp.zeros((PART, HEAD), F32)
    for distance, ref in ((3, three_ref), (2, two_ref), (1, one_ref)):
        longer = jnp.exp(ref[PART : PART + 1, :]) * state + ref[0:PART, :]
        state = jnp.where(place >= distance, longer, state)
    for distance, ref in ((1, one_ref), (2, two_ref), (3, three_ref)):
        longer = jnp.exp(ref[PART : PART + 1, :]) * trail + ref[0:PART, :]
        trail = jnp.where(place < distance, longer, trail)

    def hop(at, carry):
        state, trail = carry
        back = count - 1 - at
        out_ref[at, 0:PART, :] = state.astype(BF16)
        out_ref[back, PART : 2 * PART, :] = trail.astype(BF16)
        decay = unpack_decay(pieces_ref[at, 2 * PART :, :])
        decay_back = unpack_decay(pieces_ref[back, 2 * PART :, :])
        state = jnp.exp(decay) * state + pieces_ref[at, 0:PART, :].astype(F32)
        trail = jnp.exp(decay_back) * trail + pieces_ref[back, PART : 2 * PART, :].astype(F32)
        return state, trail

    lax.fori_loop(0, count, hop, (state, trail), unroll=8)


def other_entries(half_ref, own_ref, pair_ref, out_ref):
    first = half_ref[0] == 0
    for head in range(HALF_HEADS):
        decay = jnp.exp(unpack_decay(own_ref[head, 2 * HEAD :, :]))
        for part in range(2):
            rows = slice(part * PART, (part + 1) * PART)
            qd_rows = slice(HEAD + part * PART, HEAD + (part + 1) * PART)
            state = pair_ref[2 * head + part, 0:PART, :].astype(F32)
            trail = pair_ref[2 * head + part, PART : 2 * PART, :].astype(F32)
            later = decay * state + own_ref[head, rows, :].astype(F32)
            earlier = decay * trail + own_ref[head, qd_rows, :].astype(F32)
            out_ref[head, rows, :] = jnp.where(first, later, state).astype(BF16)
            out_ref[head, qd_rows, :] = jnp.where(first, trail, earlier).astype(BF16)


def inner_results(
    decay_ref, query_ref, key_ref, value_ref, grad_ref, att_ref, qg_ref, kg_ref, vg_ref, cols_ref, rows_ref
):
    step = pl.program_id(0)

    @pl.when(step == 0)
    def _():
        set_cumuls(decay_ref[...], cols_ref, rows_ref)

    lower = lower_triangle()
    for head in range(PER_STEP):
        cols = slice(head * HEAD, (head + 1) * HEAD)
        one = slice(head, head + 1)
        query, key, value, grad = (
            ref[:, cols] for ref in (query_ref, key_ref, value_ref, grad_ref)
        )
        spread = cols_ref[step][:, one] - rows_ref[step][one]
        weights = jnp.exp(jnp.where(lower, spread, -jnp.inf))
        probs = (dot(query, key, 1, 1) * weights).astype(BF16)
        grows = (dot(grad, value, 1, 1) * weights).astype(BF16)
        att_ref[:, cols] = dot(probs, value, 1, 0).astype(BF16)
        qg_ref[:, cols] = dot(grows, key, 1, 0).astype(BF16)
        kg_ref[:, cols] = dot(grows, query, 0, 0).astype(BF16)
        vg_ref[:, cols] = dot(probs, grad, 0, 0).astype(BF16)


def add_states(rows, inner, outs, spot, at, fwd, bwd, entering, trailing):
    cols = slice(spot * HEAD, (spot + 1) * HEAD)
    query, key, value, grad = (ref[:, cols] for ref in rows)
    terms = (
        fwd * dot(query, entering, 1, 0),
        fwd * dot(grad, entering, 1, 1),
        bwd * dot(value, trailing, 1, 1),
        bwd * dot(key, trailing, 1, 0),
    )
    for out, ref, term in zip(outs, inner, terms):
        out[:, at] = (ref[:, cols].astype(F32) + term).astype(BF16)


def result_copies(half, outs_hbm, outs, sems):
    def store(array, step):
        target = pl.multiple_of(half * WIDTH + step * SLAB, SLAB)
        return pltpu.make_async_copy(
            outs[array].at[:, step * SLAB : (step + 1) * SLAB],
            outs_hbm[array].at[:, pl.ds(target, SLAB)],
            sems.at[array, step],
        )

    return store


def own_results(half_ref, decay_ref, *refs):
    held, refs = refs[:8], refs[8:]
    pair_ref, other_ref = refs[:2]
    outs_hbm, refs = refs[2:6], refs[6:]
    away, refs = refs[:8], refs[8:]
    near, refs = refs[:8], refs[8:]
    outs, refs = refs[:4], refs[4:]
    near_sems, away_sems, out_sems = refs
    half = half_ref[0]
    first = half == 0

    def fetch(array, at):
        source = pl.multiple_of(half * WIDTH + at * LOAD, LOAD)
        return pltpu.make_async_copy(
            held[array].at[:, pl.ds(source, LOAD)],
            near[array].at[:, at * LOAD : (at + 1) * LOAD],
            near_sems.at[array, at],
        )

    def fetch_away(array):
        source = pl.multiple_of((1 - half) * WIDTH, WIDTH)
        return pltpu.make_async_copy(
            held[array].at[:, pl.ds(source, WIDTH)], away[array], away_sems.at[array]
        )

    store = result_copies(half, outs_hbm, outs, out_sems)
    for at in range(LOADS):
        for array in range(8):
            fetch(array, at).start()
    fwd, bwd, _ = column_scales(half_decay(decay_ref, half))
    for array in range(8):
        fetch_away(array).start()
    for spot in range(HALF_HEADS):
        if spot % (HALF_HEADS // LOADS) == 0:
            for array in range(8):
                fetch(array, spot // (HALF_HEADS // LOADS)).wait()
        step, head = divmod(spot, PER_STEP)
        one = slice(spot, spot + 1)
        decay = jnp.exp(unpack_decay(other_ref[spot, 2 * HEAD :, :]))
        left, right = pair_ref[2 * spot], pair_ref[2 * spot + 1]
        state = jnp.concatenate([left[0:PART], right[0:PART]], axis=0).astype(F32)
        trail = jnp.concatenate([left[PART:], right[PART:]], axis=0).astype(F32)
        later = decay * state + other_ref[spot, 0:HEAD, :].astype(F32)
        earlier = decay * trail + other_ref[spot, HEAD : 2 * HEAD, :].astype(F32)
        add_states(
            near[:4], near[4:], outs, spot, slice(spot * HEAD, (spot + 1) * HEAD),
            fwd[:, one], bwd[:, one],
            jnp.where(first, state, later).astype(BF16), jnp.where(first, earlier, trail).astype(BF16),
        )
        if head == PER_STEP - 1:
            for array in range(4):
                store(array, step).start()
    for array in range(8):
        fetch_away(array).wait()
    for step in range(STEPS):
        for array in range(4):
            store(array, step).wait()


def other_results(half_ref, decay_ref, *refs):
    away, entry_ref = refs[:8], refs[8]
    outs_hbm, refs = refs[13:17], refs[17:]
    outs, (out_sems,) = refs[:4], refs[4:]
    half = half_ref[0]
    store = result_copies(half, outs_hbm, outs, out_sems)
    fwd, bwd, _ = column_scales(half_decay(decay_ref, half))
    for spot in range(HALF_HEADS):
        step, head = divmod(spot, PER_STEP)
        one = slice(spot, spot + 1)
        entry = entry_ref[spot]
        add_states(
            away[:4], away[4:], outs, spot, slice(spot * HEAD, (spot + 1) * HEAD),
            fwd[:, one], bwd[:, one], entry[0:HEAD], entry[HEAD:],
        )
        if head == PER_STEP - 1:
            for array in range(4):
                store(array, step).start()
    for step in range(STEPS):
        for array in range(4):
            store(array, step).wait()


IN_VMEM = pl.BlockSpec(memory_space=pltpu.VMEM)
IN_HBM = pl.BlockSpec(memory_space=pl.ANY)
IN_SMEM = pl.BlockSpec(memory_space=pltpu.SMEM)
CUMULS = (
    pltpu.VMEM((2 * STEPS, BLOCK, PER_STEP), F32),
    pltpu.VMEM((2 * STEPS, PER_STEP, BLOCK), F32),
)


def once(kernel, operands, outputs, scratch=(), specs=None, out_specs=None, aliases=None):
    if specs is None:
        specs = [IN_SMEM if item.shape == (1,) else IN_VMEM for item in operands]
    return pl.pallas_call(
        kernel,
        out_shape=outputs,
        in_specs=specs,
        out_specs=out_specs or jax.tree.map(lambda _: IN_VMEM, outputs),
        scratch_shapes=list(scratch),
        input_output_aliases=aliases or {},
        compiler_params=pltpu.CompilerParams(vmem_limit_bytes=VMEM_LIMIT),
    )(*operands)


def in_hbm(item):
    return pltpu.with_memory_space_constraint(item, pltpu.HBM)


def shards(queries, key_rows, value_rows, out_grad, log_decay):
    core = lax.axis_index("core")
    mine = core.reshape(1).astype(jnp.int32)
    theirs = 1 - mine
    place = lax.axis_index("zh").reshape(1).astype(jnp.int32)
    rows = tuple(in_hbm(item) for item in (queries, key_rows, value_rows, out_grad))
    decay = log_decay.T
    decay_hbm = in_hbm(decay)
    state_rows = 2 * HEAD + TAIL
    piece_rows = 2 * PART + TAIL
    swap = [(0, 1), (1, 0)]
    states = (HALF_HEADS, state_rows, HEAD)
    pieces_shape = (2 * HALF_HEADS, piece_rows, HEAD)

    buffers = (pltpu.VMEM((BLOCK, WIDTH), BF16),)
    sent, *kept_rows = once(
        sent_states, (theirs, decay_hbm) + rows, [pltpu.VMEM(states, BF16)] + list(buffers * 4),
        buffers * 4
        + (
            pltpu.VMEM(decay.shape, BF16),
            pltpu.SemaphoreType.DMA((4, LOADS)),
            pltpu.SemaphoreType.DMA((4,)),
            pltpu.SemaphoreType.DMA((1,)),
        ),
        [IN_SMEM] + [IN_HBM] * 5,
    )
    other = lax.ppermute(sent, "core", swap)
    own, own_wide = once(
        kept_states, (mine, decay, *kept_rows), [pltpu.VMEM(states, BF16), pltpu.VMEM(states, F32)]
    )
    pairs = once(
        pair_states, (mine, own_wide, other), pltpu.HBM(pieces_shape, BF16),
        (pltpu.VMEM(pieces_shape, BF16), pltpu.SemaphoreType.DMA((STEPS,))),
        out_specs=IN_HBM,
    )
    pieces = lax.all_to_all(pairs, GROUP, split_axis=0, concat_axis=0, tiled=True)
    decay_later = lax.optimization_barrier((decay, pairs))[0]
    slab = pl.BlockSpec((BLOCK, SLAB), lambda step: (0, step))
    inner = pl.pallas_call(
        inner_results,
        out_shape=[pltpu.HBM(queries.shape, BF16)] * 4,
        grid_spec=pltpu.PrefetchScalarGridSpec(
            num_scalar_prefetch=0, grid=(2 * STEPS,),
            in_specs=[pl.BlockSpec(decay.shape, lambda step: (0, 0))] + [slab] * 4,
            out_specs=[slab] * 4, scratch_shapes=list(CUMULS),
        ),
        compiler_params=pltpu.CompilerParams(vmem_limit_bytes=VMEM_LIMIT),
    )(decay_later, *rows)
    pieces, inner = lax.optimization_barrier((pieces, inner))
    inner = tuple(in_hbm(item) for item in inner)
    size = lax.axis_size("zh")
    totals = once(group_total, (place, pieces), [pltpu.VMEM((PART + TAIL, HEAD), F32)] * (size - 1))
    moved = [
        lax.ppermute(total, "zh", [(at, (at + distance) % size) for at in range(size)])
        for distance, total in enumerate(totals, 1)
    ]
    entries = once(
        group_entries, (place, pieces, *moved), pltpu.VMEM((2 * HALF_HEADS, 2 * PART, HEAD), BF16)
    )
    pair_entries = lax.all_to_all(entries, GROUP, split_axis=0, concat_axis=0, tiled=True)
    leaving = once(
        other_entries, (mine, own, pair_entries), pltpu.VMEM((HALF_HEADS, 2 * HEAD, HEAD), BF16)
    )
    arrived = lax.ppermute(leaving, "core", swap)
    shapes = [pltpu.HBM(queries.shape, BF16)] * 4
    results = once(
        own_results, (mine, decay) + rows + inner + (pair_entries, other),
        shapes + list(buffers * 8),
        buffers * 12
        + (
            pltpu.SemaphoreType.DMA((8, LOADS)),
            pltpu.SemaphoreType.DMA((8,)),
            pltpu.SemaphoreType.DMA((4, STEPS)),
        ),
        [IN_SMEM, IN_VMEM] + [IN_HBM] * 8 + [IN_VMEM] * 2,
        [IN_HBM] * 4 + [IN_VMEM] * 8,
    )
    results = once(
        other_results, (theirs, decay) + tuple(results[4:]) + (arrived,) + tuple(results[:4]), shapes,
        buffers * 4 + (pltpu.SemaphoreType.DMA((4, STEPS)),),
        [IN_SMEM] + [IN_VMEM] * 10 + [IN_HBM] * 4, [IN_HBM] * 4,
        {11: 0, 12: 1, 13: 2, 14: 3},
    )
    return tuple(results)


def solution(mesh):
    chain, inner = mesh.devices.shape
    grid = Mesh(mesh.devices.reshape(chain // 2, 2, 4, 4, inner // 16), AXES)
    spec = P(AXES, None)
    return jax.shard_map(
        shards, mesh=grid, in_specs=(spec,) * 5, out_specs=(spec,) * 4, check_vma=False
    )
```

```python
import jax
import jax.numpy as jnp
from jax import lax
from jax.experimental import pallas as pl
from jax.experimental.pallas import tpu as pltpu
from jax.sharding import Mesh, PartitionSpec as P

HEAD = 128
BLOCK = 128
HALF_HEADS = 16
STEPS = 4
PER_STEP = HALF_HEADS // STEPS
PART = HEAD // 2
TAIL = 8
SLAB = PER_STEP * HEAD
WIDTH = HALF_HEADS * HEAD
LOADS = 2
LOAD = WIDTH // LOADS
HELD = 2
DISTANCES = (2, 1, 3)
AXES = ("zh", "zl", "y", "x", "core")
GROUP = ("zl", "y", "x")

F32 = jnp.float32
BF16 = jnp.bfloat16
VMEM_LIMIT = 16 * 1024 * 1024


def dot(left, right, left_dim, right_dim):
    return lax.dot_general(
        left, right, (((left_dim,), (right_dim,)), ((), ())), preferred_element_type=F32
    )


def pack_decay(value):
    full = jnp.broadcast_to(value, (TAIL, HEAD))
    high = full.astype(BF16)
    rest = full - high.astype(F32)
    middle = rest.astype(BF16)
    low = (rest - middle.astype(F32)).astype(BF16)
    row = lax.broadcasted_iota(jnp.int32, (TAIL, HEAD), 0)
    chosen = jnp.where(
        row == 0, high.astype(F32), jnp.where(row == 1, middle.astype(F32), low.astype(F32))
    )
    return chosen.astype(BF16)


def unpack_decay(tile):
    rows = tile.astype(F32)
    return rows[0:1] + rows[1:2] + rows[2:3]


def lower_triangle():
    at = lax.broadcasted_iota(jnp.int32, (BLOCK, BLOCK), 0)
    before = lax.broadcasted_iota(jnp.int32, (BLOCK, BLOCK), 1)
    return at >= before


def half_decay(decay_ref, half):
    decay = decay_ref[...].astype(F32)
    return jnp.where(half == 0, decay[:HALF_HEADS], decay[HALF_HEADS:]).astype(BF16)


def column_scales(decay):
    cumul = dot(lower_triangle().astype(F32).astype(BF16), decay, 1, 1)
    finals = cumul[BLOCK - 1 : BLOCK, :]
    return jnp.exp(cumul), jnp.exp(finals - cumul), finals


def set_cumuls(decay, cols_ref, rows_ref):
    triangle = lower_triangle().astype(F32).astype(BF16)
    cumul = dot(triangle, decay, 1, 1)
    rows = dot(decay, triangle, 1, 1)
    for step in range(2 * STEPS):
        heads = slice(step * PER_STEP, (step + 1) * PER_STEP)
        cols_ref[step] = cumul[:, heads]
        rows_ref[step] = rows[heads]


def head_states(query, key, value, grad, fwd, bwd):
    scaled_key = (key.astype(F32) * bwd).astype(BF16)
    scaled_query = (query.astype(F32) * fwd).astype(BF16)
    return dot(scaled_key, value, 0, 0), dot(scaled_query, grad, 0, 0)


def write_states(spot, rows, fwd, bwd, finals, outs):
    cols = slice(spot * HEAD, (spot + 1) * HEAD)
    one = slice(spot, spot + 1)
    query, key, value, grad = (ref[:, cols] for ref in rows)
    kv, qd = head_states(query, key, value, grad, fwd[:, one], bwd[:, one])
    tail = pack_decay(finals[:, one])
    for out_ref in outs:
        out_ref[spot, 0:HEAD, :] = kv.astype(out_ref.dtype)
        out_ref[spot, HEAD : 2 * HEAD, :] = qd.astype(out_ref.dtype)
        out_ref[spot, 2 * HEAD :, :] = tail.astype(out_ref.dtype)


def sent_states(half_ref, decay_hbm, *refs):
    sources, out_ref, away, rows = refs[:4], refs[4], refs[5:9], refs[9:13]
    decay_ref, sems, away_sems, decay_sem = refs[13:]
    half = half_ref[0]

    def fetch(array, at):
        source = pl.multiple_of(half * WIDTH + at * LOAD, LOAD)
        return pltpu.make_async_copy(
            sources[array].at[:, pl.ds(source, LOAD)],
            rows[array].at[:, at * LOAD : (at + 1) * LOAD],
            sems.at[array, at],
        )

    def fetch_away(array):
        source = pl.multiple_of((1 - half) * WIDTH, WIDTH)
        return pltpu.make_async_copy(
            sources[array].at[:, pl.ds(source, WIDTH)], away[array], away_sems.at[array]
        )

    decay_copy = pltpu.make_async_copy(decay_hbm, decay_ref, decay_sem.at[0])
    decay_copy.start()
    for array in range(4):
        fetch(array, 0).start()
    decay_copy.wait()
    fwd, bwd, finals = column_scales(half_decay(decay_ref, half))
    for array in range(4):
        fetch(array, 1).start()
    for spot in range(HALF_HEADS):
        if spot % (HALF_HEADS // LOADS) == 0:
            for array in range(4):
                fetch(array, spot // (HALF_HEADS // LOADS)).wait()
        if spot == PER_STEP:
            for array in range(4):
                fetch_away(array).start()
        write_states(spot, rows, fwd, bwd, finals, (out_ref,))
    for array in range(4):
        fetch_away(array).wait()


def kept_states(half_ref, decay_ref, *refs):
    rows, outs = refs[:4], refs[4:]
    fwd, bwd, finals = column_scales(half_decay(decay_ref, half_ref[0]))
    for spot in range(HALF_HEADS):
        write_states(spot, rows, fwd, bwd, finals, outs)


def pair_states(half_ref, own_ref, other_ref, out_hbm, mine_ref, their_ref, pair_ref, sems):
    kept_from = pl.multiple_of(half_ref[0] * HEAD, HEAD)
    their_from = pl.multiple_of((1 - half_ref[0]) * HEAD, HEAD)
    first = half_ref[0] == 0
    chunk = 2 * HALF_HEADS // STEPS

    def send(step):
        spots = slice(step * chunk, (step + 1) * chunk)
        return pltpu.make_async_copy(pair_ref.at[spots], out_hbm.at[spots], sems.at[step])

    for head in range(HALF_HEADS):
        mine = unpack_decay(own_ref[head, 2 * HEAD :, :])
        theirs = unpack_decay(other_ref[head, 2 * HEAD :, :])
        decay_mine = jnp.exp(mine)
        decay_theirs = jnp.exp(theirs)
        unit = jnp.ones_like(mine)
        kv_scales = (jnp.where(first, decay_theirs, unit), jnp.where(first, unit, decay_mine))
        qd_scales = (jnp.where(first, unit, decay_theirs), jnp.where(first, decay_mine, unit))
        tail = pack_decay(mine + theirs)
        for part in range(2):
            piece = 2 * head + part
            for at, (scale_own, scale_other) in ((0, kv_scales), (1, qd_scales)):
                rows = slice(at * HEAD + part * PART, at * HEAD + (part + 1) * PART)
                joined = scale_own * own_ref[head, rows, :] + scale_other * other_ref[
                    head, rows, :
                ].astype(F32)
                pair_ref[piece, at * PART : (at + 1) * PART, :] = joined.astype(BF16)
            pair_ref[piece, 2 * PART :, :] = tail
        if (head + 1) % PER_STEP == 0:
            send(head // PER_STEP).start()
    for head in range(HALF_HEADS):
        mine_ref[head, 0:HEAD, :] = own_ref[head, pl.ds(kept_from, HEAD), :].astype(BF16)
        mine_ref[head, HEAD:, :] = own_ref[head, 2 * HEAD :, :].astype(BF16)
        their_ref[head, 0:HEAD, :] = other_ref[head, pl.ds(their_from, HEAD), :]
        their_ref[head, HEAD:, :] = other_ref[head, 2 * HEAD :, :]
    for step in range(STEPS):
        send(step).wait()


def group_total(index_ref, pieces_ref, *outs):
    count = pieces_ref.shape[0]
    place = index_ref[0]
    zero = jnp.zeros((PART, HEAD), F32)

    def hop(at, carry):
        state, trail, total = carry
        back = count - 1 - at
        decay = unpack_decay(pieces_ref[at, 2 * PART :, :])
        decay_back = unpack_decay(pieces_ref[back, 2 * PART :, :])
        state = jnp.exp(decay) * state + pieces_ref[at, 0:PART, :].astype(F32)
        trail = jnp.exp(decay_back) * trail + pieces_ref[back, PART : 2 * PART, :].astype(F32)
        return state, trail, total + decay

    state, trail, total = lax.fori_loop(
        0, count, hop, (zero, zero, jnp.zeros((1, HEAD), F32)), unroll=8
    )
    tail = jnp.broadcast_to(total, (TAIL, HEAD))
    for distance, ref in zip(DISTANCES, outs):
        ref[0:PART, :] = jnp.where(place + distance <= len(outs), state, trail)
        ref[PART:, :] = tail


def group_entries(index_ref, pieces_ref, two_ref, one_ref, three_ref, out_ref):
    count = pieces_ref.shape[0]
    place = index_ref[0]
    state = jnp.zeros((PART, HEAD), F32)
    trail = jnp.zeros((PART, HEAD), F32)
    for distance, ref in ((3, three_ref), (2, two_ref), (1, one_ref)):
        longer = jnp.exp(ref[PART : PART + 1, :]) * state + ref[0:PART, :]
        state = jnp.where(place >= distance, longer, state)
    for distance, ref in ((1, one_ref), (2, two_ref), (3, three_ref)):
        longer = jnp.exp(ref[PART : PART + 1, :]) * trail + ref[0:PART, :]
        trail = jnp.where(place < distance, longer, trail)

    def hop(at, carry):
        state, trail = carry
        back = count - 1 - at
        out_ref[at, 0:PART, :] = state.astype(BF16)
        out_ref[back, PART : 2 * PART, :] = trail.astype(BF16)
        decay = unpack_decay(pieces_ref[at, 2 * PART :, :])
        decay_back = unpack_decay(pieces_ref[back, 2 * PART :, :])
        state = jnp.exp(decay) * state + pieces_ref[at, 0:PART, :].astype(F32)
        trail = jnp.exp(decay_back) * trail + pieces_ref[back, PART : 2 * PART, :].astype(F32)
        return state, trail

    lax.fori_loop(0, count, hop, (state, trail), unroll=8)


def write_entries(changed, states_ref, pair_ref, out_ref):
    step_from = pl.multiple_of(changed * PART, PART)
    same_from = pl.multiple_of((1 - changed) * PART, PART)
    for head in range(HALF_HEADS):
        decay = jnp.exp(unpack_decay(states_ref[head, HEAD:, :]))
        for part in range(2):
            lines = slice(part * PART, (part + 1) * PART)
            carried = pair_ref[2 * head + part, pl.ds(step_from, PART), :].astype(F32)
            joined = decay * carried + states_ref[head, lines, :].astype(F32)
            step_to = pl.multiple_of(changed * HEAD + part * PART, PART)
            same_to = pl.multiple_of((1 - changed) * HEAD + part * PART, PART)
            out_ref[head, pl.ds(step_to, PART), :] = joined.astype(BF16)
            out_ref[head, pl.ds(same_to, PART), :] = pair_ref[2 * head + part, pl.ds(same_from, PART), :]


def other_entries(half_ref, mine_ref, pair_ref, out_ref):
    write_entries(half_ref[0], mine_ref, pair_ref, out_ref)


def inner_results(
    decay_ref, query_ref, key_ref, value_ref, grad_ref, att_ref, qg_ref, kg_ref, vg_ref, cols_ref, rows_ref
):
    step = pl.program_id(0)

    @pl.when(step == 0)
    def _():
        set_cumuls(decay_ref[...], cols_ref, rows_ref)

    lower = lower_triangle()
    for head in range(PER_STEP):
        cols = slice(head * HEAD, (head + 1) * HEAD)
        one = slice(head, head + 1)
        query, key, value, grad = (
            ref[:, cols] for ref in (query_ref, key_ref, value_ref, grad_ref)
        )
        spread = cols_ref[step][:, one] - rows_ref[step][one]
        weights = jnp.exp(jnp.where(lower, spread, -jnp.inf))
        probs = (dot(query, key, 1, 1) * weights).astype(BF16)
        grows = (dot(grad, value, 1, 1) * weights).astype(BF16)
        att_ref[:, cols] = dot(probs, value, 1, 0).astype(BF16)
        qg_ref[:, cols] = dot(grows, key, 1, 0).astype(BF16)
        kg_ref[:, cols] = dot(grows, query, 0, 0).astype(BF16)
        vg_ref[:, cols] = dot(probs, grad, 0, 0).astype(BF16)


def add_states(rows, inner, outs, spot, at, fwd, bwd, entering, trailing):
    cols = slice(spot * HEAD, (spot + 1) * HEAD)
    query, key, value, grad = (ref[:, cols] for ref in rows)
    terms = (
        fwd * dot(query, entering, 1, 0),
        fwd * dot(grad, entering, 1, 1),
        bwd * dot(value, trailing, 1, 1),
        bwd * dot(key, trailing, 1, 0),
    )
    for out, ref, term in zip(outs, inner, terms):
        out[:, at] = (ref[:, cols].astype(F32) + term).astype(BF16)


def result_copies(half, outs_hbm, outs, sems):
    def store(array, step):
        target = pl.multiple_of(half * WIDTH + step * SLAB, SLAB)
        return pltpu.make_async_copy(
            outs[array].at[:, step * SLAB : (step + 1) * SLAB],
            outs_hbm[array].at[:, pl.ds(target, SLAB)],
            sems.at[array, step],
        )

    return store


def own_results(half_ref, decay_ref, *refs):
    held, refs = refs[:8], refs[8:]
    near, (pair_ref, their_ref), refs = refs[:HELD], refs[HELD : HELD + 2], refs[HELD + 2 :]
    outs_hbm, refs = refs[:4], refs[4:]
    away, refs = refs[:8], refs[8:]
    near, refs = near + refs[: 8 - HELD], refs[8 - HELD :]
    outs, refs = refs[:4], refs[4:]
    entry_ref, near_sems, away_sems, out_sems = refs
    half = half_ref[0]

    def fetch(array, at):
        source = pl.multiple_of(half * WIDTH + at * LOAD, LOAD)
        return pltpu.make_async_copy(
            held[array].at[:, pl.ds(source, LOAD)],
            near[array].at[:, at * LOAD : (at + 1) * LOAD],
            near_sems.at[array, at],
        )

    def fetch_away(array):
        source = pl.multiple_of((1 - half) * WIDTH, WIDTH)
        return pltpu.make_async_copy(
            held[array].at[:, pl.ds(source, WIDTH)], away[array], away_sems.at[array]
        )

    store = result_copies(half, outs_hbm, outs, out_sems)
    for array in range(HELD, 8):
        fetch(array, 0).start()
    fwd, bwd, _ = column_scales(half_decay(decay_ref, half))
    write_entries(1 - half, their_ref, pair_ref, entry_ref)
    for array in range(HELD, 8):
        fetch(array, 1).start()
    for spot in range(HALF_HEADS):
        if spot % (HALF_HEADS // LOADS) == 0:
            for array in range(HELD, 8):
                fetch(array, spot // (HALF_HEADS // LOADS)).wait()
        if spot == PER_STEP:
            for array in range(8):
                fetch_away(array).start()
        step, head = divmod(spot, PER_STEP)
        one = slice(spot, spot + 1)
        entry = entry_ref[spot]
        add_states(
            near[:4], near[4:], outs, spot, slice(spot * HEAD, (spot + 1) * HEAD),
            fwd[:, one], bwd[:, one], entry[0:HEAD], entry[HEAD:],
        )
        if head == PER_STEP - 1:
            for array in range(4):
                store(array, step).start()
    for array in range(8):
        fetch_away(array).wait()
    for step in range(STEPS):
        for array in range(4):
            store(array, step).wait()


def other_results(half_ref, decay_ref, *refs):
    away, entry_ref = refs[:8], refs[8]
    outs_hbm, refs = refs[13:17], refs[17:]
    outs, (out_sems,) = refs[:4], refs[4:]
    half = half_ref[0]
    store = result_copies(half, outs_hbm, outs, out_sems)
    fwd, bwd, _ = column_scales(half_decay(decay_ref, half))
    for spot in range(HALF_HEADS):
        step, head = divmod(spot, PER_STEP)
        one = slice(spot, spot + 1)
        entry = entry_ref[spot]
        add_states(
            away[:4], away[4:], outs, spot, slice(spot * HEAD, (spot + 1) * HEAD),
            fwd[:, one], bwd[:, one], entry[0:HEAD], entry[HEAD:],
        )
        if head == PER_STEP - 1:
            for array in range(4):
                store(array, step).start()
    for step in range(STEPS):
        for array in range(4):
            store(array, step).wait()


IN_VMEM = pl.BlockSpec(memory_space=pltpu.VMEM)
IN_HBM = pl.BlockSpec(memory_space=pl.ANY)
IN_SMEM = pl.BlockSpec(memory_space=pltpu.SMEM)
CUMULS = (
    pltpu.VMEM((2 * STEPS, BLOCK, PER_STEP), F32),
    pltpu.VMEM((2 * STEPS, PER_STEP, BLOCK), F32),
)


def once(kernel, operands, outputs, scratch=(), specs=None, out_specs=None, aliases=None):
    if specs is None:
        specs = [IN_SMEM if item.shape == (1,) else IN_VMEM for item in operands]
    return pl.pallas_call(
        kernel,
        out_shape=outputs,
        in_specs=specs,
        out_specs=out_specs or jax.tree.map(lambda _: IN_VMEM, outputs),
        scratch_shapes=list(scratch),
        input_output_aliases=aliases or {},
        compiler_params=pltpu.CompilerParams(vmem_limit_bytes=VMEM_LIMIT),
    )(*operands)


def in_hbm(item):
    return pltpu.with_memory_space_constraint(item, pltpu.HBM)


def shards(queries, key_rows, value_rows, out_grad, log_decay):
    core = lax.axis_index("core")
    mine = core.reshape(1).astype(jnp.int32)
    theirs = 1 - mine
    place = lax.axis_index("zh").reshape(1).astype(jnp.int32)
    rows = tuple(in_hbm(item) for item in (queries, key_rows, value_rows, out_grad))
    decay = log_decay.T
    decay_hbm = in_hbm(decay)
    state_rows = 2 * HEAD + TAIL
    piece_rows = 2 * PART + TAIL
    swap = [(0, 1), (1, 0)]
    states = (HALF_HEADS, state_rows, HEAD)
    pieces_shape = (2 * HALF_HEADS, piece_rows, HEAD)

    buffers = (pltpu.VMEM((BLOCK, WIDTH), BF16),)
    sent, *kept_rows = once(
        sent_states, (theirs, decay_hbm) + rows, [pltpu.VMEM(states, BF16)] + list(buffers * 4),
        buffers * 4
        + (
            pltpu.VMEM(decay.shape, BF16),
            pltpu.SemaphoreType.DMA((4, LOADS)),
            pltpu.SemaphoreType.DMA((4,)),
            pltpu.SemaphoreType.DMA((1,)),
        ),
        [IN_SMEM] + [IN_HBM] * 5,
    )
    other = lax.ppermute(sent, "core", swap)
    (own,) = once(kept_states, (mine, decay, *kept_rows), [pltpu.VMEM(states, F32)])
    part_states = pltpu.VMEM((HALF_HEADS, HEAD + TAIL, HEAD), BF16)
    pairs, own_part, other_part = once(
        pair_states, (mine, own, other), [pltpu.HBM(pieces_shape, BF16), part_states, part_states],
        (pltpu.VMEM(pieces_shape, BF16), pltpu.SemaphoreType.DMA((STEPS,))),
        out_specs=[IN_HBM, IN_VMEM, IN_VMEM],
    )
    pieces = lax.all_to_all(pairs, GROUP, split_axis=0, concat_axis=0, tiled=True)
    decay_later = lax.optimization_barrier((decay, pairs))[0]
    slab = pl.BlockSpec((BLOCK, SLAB), lambda step: (0, step))
    inner = pl.pallas_call(
        inner_results,
        out_shape=[pltpu.HBM(queries.shape, BF16)] * 4,
        grid_spec=pltpu.PrefetchScalarGridSpec(
            num_scalar_prefetch=0, grid=(2 * STEPS,),
            in_specs=[pl.BlockSpec(decay.shape, lambda step: (0, 0))] + [slab] * 4,
            out_specs=[slab] * 4, scratch_shapes=list(CUMULS),
        ),
        compiler_params=pltpu.CompilerParams(vmem_limit_bytes=VMEM_LIMIT),
    )(decay_later, *rows)
    pieces, inner = lax.optimization_barrier((pieces, inner))
    inner = tuple(in_hbm(item) for item in inner)
    size = lax.axis_size("zh")
    totals = once(group_total, (place, pieces), [pltpu.VMEM((PART + TAIL, HEAD), F32)] * (size - 1))
    moved = [
        lax.ppermute(total, "zh", [(at, (at + distance) % size) for at in range(size)])
        for distance, total in zip(DISTANCES, totals)
    ]
    entries = once(
        group_entries, (place, pieces, *moved), pltpu.VMEM((2 * HALF_HEADS, 2 * PART, HEAD), BF16)
    )
    pair_entries = lax.all_to_all(entries, GROUP, split_axis=0, concat_axis=0, tiled=True)
    leaving = once(
        other_entries, (mine, own_part, pair_entries), pltpu.VMEM((HALF_HEADS, 2 * HEAD, HEAD), BF16)
    )
    arrived = lax.ppermute(leaving, "core", swap)
    shapes = [pltpu.HBM(queries.shape, BF16)] * 4
    results = once(
        own_results, (mine, decay) + rows + inner + tuple(kept_rows[:HELD]) + (pair_entries, other_part),
        shapes + list(buffers * 8),
        buffers * (12 - HELD)
        + (
            pltpu.VMEM((HALF_HEADS, 2 * HEAD, HEAD), BF16),
            pltpu.SemaphoreType.DMA((8, LOADS)),
            pltpu.SemaphoreType.DMA((8,)),
            pltpu.SemaphoreType.DMA((4, STEPS)),
        ),
        [IN_SMEM, IN_VMEM] + [IN_HBM] * 8 + [IN_VMEM] * (2 + HELD),
        [IN_HBM] * 4 + [IN_VMEM] * 8,
    )
    results = once(
        other_results, (theirs, decay) + tuple(results[4:]) + (arrived,) + tuple(results[:4]), shapes,
        buffers * 4 + (pltpu.SemaphoreType.DMA((4, STEPS)),),
        [IN_SMEM] + [IN_VMEM] * 10 + [IN_HBM] * 4, [IN_HBM] * 4,
        {11: 0, 12: 1, 13: 2, 14: 3},
    )
    return tuple(results)


def solution(mesh):
    chain, inner = mesh.devices.shape
    grid = Mesh(mesh.devices.reshape(chain // 2, 2, 4, 4, inner // 16), AXES)
    spec = P(AXES, None)
    return jax.shard_map(
        shards, mesh=grid, in_specs=(spec,) * 5, out_specs=(spec,) * 4, check_vma=False
    )
```

```python
import jax
import jax.numpy as jnp
from jax import lax
from jax.experimental import pallas as pl
from jax.experimental.pallas import tpu as pltpu
from jax.sharding import Mesh, PartitionSpec as P

HEAD = 128
BLOCK = 128
HALF_HEADS = 16
STEPS = 4
PER_STEP = HALF_HEADS // STEPS
PART = HEAD // 2
TAIL = 8
SLAB = PER_STEP * HEAD
WIDTH = HALF_HEADS * HEAD
LOADS = 2
LOAD = WIDTH // LOADS
HELD = 2
DISTANCES = (2, 1, 3)
AXES = ("zh", "zl", "y", "x", "core")
GROUP = ("zl", "y", "x")

F32 = jnp.float32
BF16 = jnp.bfloat16
VMEM_LIMIT = 16 * 1024 * 1024


def dot(left, right, left_dim, right_dim):
    return lax.dot_general(
        left, right, (((left_dim,), (right_dim,)), ((), ())), preferred_element_type=F32
    )


def pack_decay(value):
    full = jnp.broadcast_to(value, (TAIL, HEAD))
    high = full.astype(BF16)
    rest = full - high.astype(F32)
    middle = rest.astype(BF16)
    low = (rest - middle.astype(F32)).astype(BF16)
    row = lax.broadcasted_iota(jnp.int32, (TAIL, HEAD), 0)
    chosen = jnp.where(
        row == 0, high.astype(F32), jnp.where(row == 1, middle.astype(F32), low.astype(F32))
    )
    return chosen.astype(BF16)


def unpack_decay(tile):
    rows = tile.astype(F32)
    return rows[0:1] + rows[1:2] + rows[2:3]


def lower_triangle():
    at = lax.broadcasted_iota(jnp.int32, (BLOCK, BLOCK), 0)
    before = lax.broadcasted_iota(jnp.int32, (BLOCK, BLOCK), 1)
    return at >= before


def half_decay(decay_ref, half):
    decay = decay_ref[...].astype(F32)
    return jnp.where(half == 0, decay[:HALF_HEADS], decay[HALF_HEADS:]).astype(BF16)


def column_scales(decay):
    cumul = dot(lower_triangle().astype(F32).astype(BF16), decay, 1, 1)
    finals = cumul[BLOCK - 1 : BLOCK, :]
    return jnp.exp(cumul), jnp.exp(finals - cumul), finals


def set_cumuls(decay, cols_ref, rows_ref):
    triangle = lower_triangle().astype(F32).astype(BF16)
    cumul = dot(triangle, decay, 1, 1)
    rows = dot(decay, triangle, 1, 1)
    for step in range(2 * STEPS):
        heads = slice(step * PER_STEP, (step + 1) * PER_STEP)
        cols_ref[step] = cumul[:, heads]
        rows_ref[step] = rows[heads]


def head_states(query, key, value, grad, fwd, bwd):
    scaled_key = (key.astype(F32) * bwd).astype(BF16)
    scaled_query = (query.astype(F32) * fwd).astype(BF16)
    return dot(scaled_key, value, 0, 0), dot(scaled_query, grad, 0, 0)


def write_states(spot, rows, fwd, bwd, finals, outs):
    cols = slice(spot * HEAD, (spot + 1) * HEAD)
    one = slice(spot, spot + 1)
    query, key, value, grad = (ref[:, cols] for ref in rows)
    kv, qd = head_states(query, key, value, grad, fwd[:, one], bwd[:, one])
    tail = pack_decay(finals[:, one])
    for out_ref in outs:
        out_ref[spot, 0:HEAD, :] = kv.astype(out_ref.dtype)
        out_ref[spot, HEAD : 2 * HEAD, :] = qd.astype(out_ref.dtype)
        out_ref[spot, 2 * HEAD :, :] = tail.astype(out_ref.dtype)


def sent_states(half_ref, decay_hbm, *refs):
    sources, out_ref, away, rows = refs[:4], refs[4], refs[5:9], refs[9:13]
    decay_ref, sems, away_sems, decay_sem = refs[13:]
    half = half_ref[0]

    def fetch(array, at):
        source = pl.multiple_of(half * WIDTH + at * LOAD, LOAD)
        return pltpu.make_async_copy(
            sources[array].at[:, pl.ds(source, LOAD)],
            rows[array].at[:, at * LOAD : (at + 1) * LOAD],
            sems.at[array, at],
        )

    def fetch_away(array):
        source = pl.multiple_of((1 - half) * WIDTH, WIDTH)
        return pltpu.make_async_copy(
            sources[array].at[:, pl.ds(source, WIDTH)], away[array], away_sems.at[array]
        )

    decay_copy = pltpu.make_async_copy(decay_hbm, decay_ref, decay_sem.at[0])
    decay_copy.start()
    for array in range(4):
        fetch(array, 0).start()
    decay_copy.wait()
    fwd, bwd, finals = column_scales(half_decay(decay_ref, half))
    for array in range(4):
        fetch(array, 1).start()
    for spot in range(HALF_HEADS):
        if spot % (HALF_HEADS // LOADS) == 0:
            for array in range(4):
                fetch(array, spot // (HALF_HEADS // LOADS)).wait()
        if spot == PER_STEP:
            for array in range(4):
                fetch_away(array).start()
        write_states(spot, rows, fwd, bwd, finals, (out_ref,))
    for array in range(4):
        fetch_away(array).wait()


def kept_states(half_ref, decay_ref, *refs):
    rows, outs = refs[:4], refs[4:]
    fwd, bwd, finals = column_scales(half_decay(decay_ref, half_ref[0]))
    for spot in range(HALF_HEADS):
        write_states(spot, rows, fwd, bwd, finals, outs)


def pair_states(half_ref, own_ref, other_ref, out_hbm, mine_ref, their_ref, pair_ref, sems):
    kept_from = pl.multiple_of(half_ref[0] * HEAD, HEAD)
    their_from = pl.multiple_of((1 - half_ref[0]) * HEAD, HEAD)
    first = half_ref[0] == 0
    chunk = 2 * HALF_HEADS // STEPS

    def send(step):
        spots = slice(step * chunk, (step + 1) * chunk)
        return pltpu.make_async_copy(pair_ref.at[spots], out_hbm.at[spots], sems.at[step])

    for head in range(HALF_HEADS):
        mine = unpack_decay(own_ref[head, 2 * HEAD :, :])
        theirs = unpack_decay(other_ref[head, 2 * HEAD :, :])
        decay_mine = jnp.exp(mine)
        decay_theirs = jnp.exp(theirs)
        unit = jnp.ones_like(mine)
        kv_scales = (jnp.where(first, decay_theirs, unit), jnp.where(first, unit, decay_mine))
        qd_scales = (jnp.where(first, unit, decay_theirs), jnp.where(first, decay_mine, unit))
        tail = pack_decay(mine + theirs)
        for part in range(2):
            piece = 2 * head + part
            for at, (scale_own, scale_other) in ((0, kv_scales), (1, qd_scales)):
                rows = slice(at * HEAD + part * PART, at * HEAD + (part + 1) * PART)
                joined = scale_own * own_ref[head, rows, :] + scale_other * other_ref[
                    head, rows, :
                ].astype(F32)
                pair_ref[piece, at * PART : (at + 1) * PART, :] = joined.astype(BF16)
            pair_ref[piece, 2 * PART :, :] = tail
        if (head + 1) % PER_STEP == 0:
            send(head // PER_STEP).start()
    for head in range(HALF_HEADS):
        mine_ref[head, 0:HEAD, :] = own_ref[head, pl.ds(kept_from, HEAD), :].astype(BF16)
        mine_ref[head, HEAD:, :] = own_ref[head, 2 * HEAD :, :].astype(BF16)
        their_ref[head, 0:HEAD, :] = other_ref[head, pl.ds(their_from, HEAD), :]
        their_ref[head, HEAD:, :] = other_ref[head, 2 * HEAD :, :]
    for step in range(STEPS):
        send(step).wait()


def group_total(index_ref, pieces_ref, *outs):
    count = pieces_ref.shape[0]
    place = index_ref[0]
    zero = jnp.zeros((PART, HEAD), F32)

    def hop(at, carry):
        state, trail, total = carry
        back = count - 1 - at
        decay = unpack_decay(pieces_ref[at, 2 * PART :, :])
        decay_back = unpack_decay(pieces_ref[back, 2 * PART :, :])
        state = jnp.exp(decay) * state + pieces_ref[at, 0:PART, :].astype(F32)
        trail = jnp.exp(decay_back) * trail + pieces_ref[back, PART : 2 * PART, :].astype(F32)
        return state, trail, total + decay

    state, trail, total = lax.fori_loop(
        0, count, hop, (zero, zero, jnp.zeros((1, HEAD), F32)), unroll=8
    )
    tail = jnp.broadcast_to(total, (TAIL, HEAD))
    for distance, ref in zip(DISTANCES, outs):
        ref[0:PART, :] = jnp.where(place + distance <= len(outs), state, trail)
        ref[PART:, :] = tail


def group_entries(index_ref, pieces_ref, two_ref, one_ref, three_ref, out_ref):
    count = pieces_ref.shape[0]
    place = index_ref[0]
    state = jnp.zeros((PART, HEAD), F32)
    trail = jnp.zeros((PART, HEAD), F32)
    for distance, ref in ((3, three_ref), (2, two_ref), (1, one_ref)):
        longer = jnp.exp(ref[PART : PART + 1, :]) * state + ref[0:PART, :]
        state = jnp.where(place >= distance, longer, state)
    for distance, ref in ((1, one_ref), (2, two_ref), (3, three_ref)):
        longer = jnp.exp(ref[PART : PART + 1, :]) * trail + ref[0:PART, :]
        trail = jnp.where(place < distance, longer, trail)

    def hop(at, carry):
        state, trail = carry
        back = count - 1 - at
        out_ref[at, 0:PART, :] = state.astype(BF16)
        out_ref[back, PART : 2 * PART, :] = trail.astype(BF16)
        decay = unpack_decay(pieces_ref[at, 2 * PART :, :])
        decay_back = unpack_decay(pieces_ref[back, 2 * PART :, :])
        state = jnp.exp(decay) * state + pieces_ref[at, 0:PART, :].astype(F32)
        trail = jnp.exp(decay_back) * trail + pieces_ref[back, PART : 2 * PART, :].astype(F32)
        return state, trail

    lax.fori_loop(0, count, hop, (state, trail), unroll=8)


def write_entries(changed, states_ref, pair_ref, out_ref):
    step_from = pl.multiple_of(changed * PART, PART)
    same_from = pl.multiple_of((1 - changed) * PART, PART)
    for head in range(HALF_HEADS):
        decay = jnp.exp(unpack_decay(states_ref[head, HEAD:, :]))
        for part in range(2):
            lines = slice(part * PART, (part + 1) * PART)
            carried = pair_ref[2 * head + part, pl.ds(step_from, PART), :].astype(F32)
            joined = decay * carried + states_ref[head, lines, :].astype(F32)
            step_to = pl.multiple_of(changed * HEAD + part * PART, PART)
            same_to = pl.multiple_of((1 - changed) * HEAD + part * PART, PART)
            out_ref[head, pl.ds(step_to, PART), :] = joined.astype(BF16)
            out_ref[head, pl.ds(same_to, PART), :] = pair_ref[2 * head + part, pl.ds(same_from, PART), :]


def other_entries(half_ref, mine_ref, pair_ref, out_ref):
    write_entries(half_ref[0], mine_ref, pair_ref, out_ref)


def inner_results(
    decay_ref, query_ref, key_ref, value_ref, grad_ref, att_ref, qg_ref, kg_ref, vg_ref, cols_ref, rows_ref
):
    step = pl.program_id(0)

    @pl.when(step == 0)
    def _():
        set_cumuls(decay_ref[...], cols_ref, rows_ref)

    lower = lower_triangle()
    for head in range(PER_STEP):
        cols = slice(head * HEAD, (head + 1) * HEAD)
        one = slice(head, head + 1)
        query, key, value, grad = (
            ref[:, cols] for ref in (query_ref, key_ref, value_ref, grad_ref)
        )
        spread = cols_ref[step][:, one] - rows_ref[step][one]
        weights = jnp.exp(jnp.where(lower, spread, -jnp.inf))
        probs = (dot(query, key, 1, 1) * weights).astype(BF16)
        grows = (dot(grad, value, 1, 1) * weights).astype(BF16)
        att_ref[:, cols] = dot(probs, value, 1, 0).astype(BF16)
        qg_ref[:, cols] = dot(grows, key, 1, 0).astype(BF16)
        kg_ref[:, cols] = dot(grows, query, 0, 0).astype(BF16)
        vg_ref[:, cols] = dot(probs, grad, 0, 0).astype(BF16)


def add_states(rows, inner, outs, spot, at, fwd, bwd, entering, trailing):
    cols = slice(spot * HEAD, (spot + 1) * HEAD)
    query, key, value, grad = (ref[:, cols] for ref in rows)
    terms = (
        fwd * dot(query, entering, 1, 0),
        fwd * dot(grad, entering, 1, 1),
        bwd * dot(value, trailing, 1, 1),
        bwd * dot(key, trailing, 1, 0),
    )
    for out, ref, term in zip(outs, inner, terms):
        out[:, at] = (ref[:, cols].astype(F32) + term).astype(BF16)


def result_copies(half, outs_hbm, outs, sems):
    def store(array, step):
        target = pl.multiple_of(half * WIDTH + step * SLAB, SLAB)
        return pltpu.make_async_copy(
            outs[array].at[:, step * SLAB : (step + 1) * SLAB],
            outs_hbm[array].at[:, pl.ds(target, SLAB)],
            sems.at[array, step],
        )

    return store


def own_results(half_ref, decay_ref, *refs):
    held, refs = refs[:8], refs[8:]
    near, (pair_ref, their_ref), refs = refs[:HELD], refs[HELD : HELD + 2], refs[HELD + 2 :]
    outs, refs = refs[:4], refs[4:]
    away, refs = refs[:8], refs[8:]
    near, refs = near + refs[: 8 - HELD], refs[8 - HELD :]
    entry_ref, near_sems, away_sems = refs
    half = half_ref[0]

    def fetch(array, at):
        source = pl.multiple_of(half * WIDTH + at * LOAD, LOAD)
        return pltpu.make_async_copy(
            held[array].at[:, pl.ds(source, LOAD)],
            near[array].at[:, at * LOAD : (at + 1) * LOAD],
            near_sems.at[array, at],
        )

    def fetch_away(array):
        source = pl.multiple_of((1 - half) * WIDTH, WIDTH)
        return pltpu.make_async_copy(
            held[array].at[:, pl.ds(source, WIDTH)], away[array], away_sems.at[array]
        )

    for array in range(HELD, 8):
        fetch(array, 0).start()
    fwd, bwd, _ = column_scales(half_decay(decay_ref, half))
    write_entries(1 - half, their_ref, pair_ref, entry_ref)
    for array in range(HELD, 8):
        fetch(array, 1).start()
    for spot in range(HALF_HEADS):
        if spot % (HALF_HEADS // LOADS) == 0:
            for array in range(HELD, 8):
                fetch(array, spot // (HALF_HEADS // LOADS)).wait()
        if spot == PER_STEP:
            for array in range(8):
                fetch_away(array).start()
        one = slice(spot, spot + 1)
        entry = entry_ref[spot]
        add_states(
            near[:4], near[4:], outs, spot, slice(spot * HEAD, (spot + 1) * HEAD),
            fwd[:, one], bwd[:, one], entry[0:HEAD], entry[HEAD:],
        )
    for array in range(8):
        fetch_away(array).wait()


def other_results(half_ref, decay_ref, *refs):
    away, entry_ref, ready = refs[:8], refs[8], refs[9:13]
    outs_hbm, outs, (out_sems, ready_sems) = refs[13:17], refs[17:21], refs[21:]
    half = half_ref[0]
    store = result_copies(half, outs_hbm, outs, out_sems)

    def store_ready(array):
        target = pl.multiple_of((1 - half) * WIDTH, WIDTH)
        return pltpu.make_async_copy(
            ready[array], outs_hbm[array].at[:, pl.ds(target, WIDTH)], ready_sems.at[array]
        )

    for array in range(4):
        store_ready(array).start()
    fwd, bwd, _ = column_scales(half_decay(decay_ref, half))
    for spot in range(HALF_HEADS):
        step, head = divmod(spot, PER_STEP)
        one = slice(spot, spot + 1)
        entry = entry_ref[spot]
        add_states(
            away[:4], away[4:], outs, spot, slice(spot * HEAD, (spot + 1) * HEAD),
            fwd[:, one], bwd[:, one], entry[0:HEAD], entry[HEAD:],
        )
        if head == PER_STEP - 1:
            for array in range(4):
                store(array, step).start()
    for array in range(4):
        store_ready(array).wait()
    for step in range(STEPS):
        for array in range(4):
            store(array, step).wait()


IN_VMEM = pl.BlockSpec(memory_space=pltpu.VMEM)
IN_HBM = pl.BlockSpec(memory_space=pl.ANY)
IN_SMEM = pl.BlockSpec(memory_space=pltpu.SMEM)
CUMULS = (
    pltpu.VMEM((2 * STEPS, BLOCK, PER_STEP), F32),
    pltpu.VMEM((2 * STEPS, PER_STEP, BLOCK), F32),
)


def once(kernel, operands, outputs, scratch=(), specs=None, out_specs=None, aliases=None):
    if specs is None:
        specs = [IN_SMEM if item.shape == (1,) else IN_VMEM for item in operands]
    return pl.pallas_call(
        kernel,
        out_shape=outputs,
        in_specs=specs,
        out_specs=out_specs or jax.tree.map(lambda _: IN_VMEM, outputs),
        scratch_shapes=list(scratch),
        input_output_aliases=aliases or {},
        compiler_params=pltpu.CompilerParams(vmem_limit_bytes=VMEM_LIMIT),
    )(*operands)


def in_hbm(item):
    return pltpu.with_memory_space_constraint(item, pltpu.HBM)


def shards(queries, key_rows, value_rows, out_grad, log_decay):
    core = lax.axis_index("core")
    mine = core.reshape(1).astype(jnp.int32)
    theirs = 1 - mine
    place = lax.axis_index("zh").reshape(1).astype(jnp.int32)
    rows = tuple(in_hbm(item) for item in (queries, key_rows, value_rows, out_grad))
    decay = log_decay.T
    decay_hbm = in_hbm(decay)
    state_rows = 2 * HEAD + TAIL
    piece_rows = 2 * PART + TAIL
    swap = [(0, 1), (1, 0)]
    states = (HALF_HEADS, state_rows, HEAD)
    pieces_shape = (2 * HALF_HEADS, piece_rows, HEAD)

    buffers = (pltpu.VMEM((BLOCK, WIDTH), BF16),)
    sent, *kept_rows = once(
        sent_states, (theirs, decay_hbm) + rows, [pltpu.VMEM(states, BF16)] + list(buffers * 4),
        buffers * 4
        + (
            pltpu.VMEM(decay.shape, BF16),
            pltpu.SemaphoreType.DMA((4, LOADS)),
            pltpu.SemaphoreType.DMA((4,)),
            pltpu.SemaphoreType.DMA((1,)),
        ),
        [IN_SMEM] + [IN_HBM] * 5,
    )
    other = lax.ppermute(sent, "core", swap)
    (own,) = once(kept_states, (mine, decay, *kept_rows), [pltpu.VMEM(states, F32)])
    part_states = pltpu.VMEM((HALF_HEADS, HEAD + TAIL, HEAD), BF16)
    pairs, own_part, other_part = once(
        pair_states, (mine, own, other), [pltpu.HBM(pieces_shape, BF16), part_states, part_states],
        (pltpu.VMEM(pieces_shape, BF16), pltpu.SemaphoreType.DMA((STEPS,))),
        out_specs=[IN_HBM, IN_VMEM, IN_VMEM],
    )
    pieces = lax.all_to_all(pairs, GROUP, split_axis=0, concat_axis=0, tiled=True)
    decay_later = lax.optimization_barrier((decay, pairs))[0]
    slab = pl.BlockSpec((BLOCK, SLAB), lambda step: (0, step))
    inner = pl.pallas_call(
        inner_results,
        out_shape=[pltpu.HBM(queries.shape, BF16)] * 4,
        grid_spec=pltpu.PrefetchScalarGridSpec(
            num_scalar_prefetch=0, grid=(2 * STEPS,),
            in_specs=[pl.BlockSpec(decay.shape, lambda step: (0, 0))] + [slab] * 4,
            out_specs=[slab] * 4, scratch_shapes=list(CUMULS),
        ),
        compiler_params=pltpu.CompilerParams(vmem_limit_bytes=VMEM_LIMIT),
    )(decay_later, *rows)
    pieces, inner = lax.optimization_barrier((pieces, inner))
    inner = tuple(in_hbm(item) for item in inner)
    size = lax.axis_size("zh")
    totals = once(group_total, (place, pieces), [pltpu.VMEM((PART + TAIL, HEAD), F32)] * (size - 1))
    moved = [
        lax.ppermute(total, "zh", [(at, (at + distance) % size) for at in range(size)])
        for distance, total in zip(DISTANCES, totals)
    ]
    entries = once(
        group_entries, (place, pieces, *moved), pltpu.VMEM((2 * HALF_HEADS, 2 * PART, HEAD), BF16)
    )
    pair_entries = lax.all_to_all(entries, GROUP, split_axis=0, concat_axis=0, tiled=True)
    leaving = once(
        other_entries, (mine, own_part, pair_entries), pltpu.VMEM((HALF_HEADS, 2 * HEAD, HEAD), BF16)
    )
    arrived = lax.ppermute(leaving, "core", swap)
    results = once(
        own_results, (mine, decay) + rows + inner + tuple(kept_rows[:HELD]) + (pair_entries, other_part),
        list(buffers * 12),
        buffers * (8 - HELD)
        + (
            pltpu.VMEM((HALF_HEADS, 2 * HEAD, HEAD), BF16),
            pltpu.SemaphoreType.DMA((8, LOADS)),
            pltpu.SemaphoreType.DMA((8,)),
        ),
        [IN_SMEM, IN_VMEM] + [IN_HBM] * 8 + [IN_VMEM] * (2 + HELD),
    )
    results = once(
        other_results, (theirs, decay) + tuple(results[4:]) + (arrived,) + tuple(results[:4]),
        [pltpu.HBM(queries.shape, BF16)] * 4,
        buffers * 4 + (pltpu.SemaphoreType.DMA((4, STEPS)), pltpu.SemaphoreType.DMA((4,))),
        out_specs=[IN_HBM] * 4,
    )
    return tuple(results)


def solution(mesh):
    chain, inner = mesh.devices.shape
    grid = Mesh(mesh.devices.reshape(chain // 2, 2, 4, 4, inner // 16), AXES)
    spec = P(AXES, None)
    return jax.shard_map(
        shards, mesh=grid, in_specs=(spec,) * 5, out_specs=(spec,) * 4, check_vma=False
    )
```

```python
import jax
import jax.numpy as jnp
from jax import lax
from jax.experimental import pallas as pl
from jax.experimental.pallas import tpu as pltpu
from jax.sharding import Mesh, PartitionSpec as P

HEAD = 128
BLOCK = 128
HALF_HEADS = 16
STEPS = 4
PER_STEP = HALF_HEADS // STEPS
PART = HEAD // 2
TAIL = 8
SLAB = PER_STEP * HEAD
WIDTH = HALF_HEADS * HEAD
LOADS = 2
LOAD = WIDTH // LOADS
HELD = 2
DISTANCES = (2, 1, 3)
AXES = ("zh", "zl", "y", "x", "core")
GROUP = ("zl", "y", "x")

F32 = jnp.float32
BF16 = jnp.bfloat16
VMEM_LIMIT = 16 * 1024 * 1024


def dot(left, right, left_dim, right_dim):
    return lax.dot_general(
        left, right, (((left_dim,), (right_dim,)), ((), ())), preferred_element_type=F32
    )


def pack_decay(value):
    full = jnp.broadcast_to(value, (TAIL, HEAD))
    high = full.astype(BF16)
    rest = full - high.astype(F32)
    middle = rest.astype(BF16)
    low = (rest - middle.astype(F32)).astype(BF16)
    row = lax.broadcasted_iota(jnp.int32, (TAIL, HEAD), 0)
    chosen = jnp.where(
        row == 0, high.astype(F32), jnp.where(row == 1, middle.astype(F32), low.astype(F32))
    )
    return chosen.astype(BF16)


def unpack_decay(tile):
    rows = tile.astype(F32)
    return rows[0:1] + rows[1:2] + rows[2:3]


def lower_triangle():
    at = lax.broadcasted_iota(jnp.int32, (BLOCK, BLOCK), 0)
    before = lax.broadcasted_iota(jnp.int32, (BLOCK, BLOCK), 1)
    return at >= before


def half_decay(decay_ref, half):
    decay = decay_ref[...].astype(F32)
    return jnp.where(half == 0, decay[:HALF_HEADS], decay[HALF_HEADS:]).astype(BF16)


def column_scales(decay):
    cumul = dot(lower_triangle().astype(F32).astype(BF16), decay, 1, 1)
    finals = cumul[BLOCK - 1 : BLOCK, :]
    return jnp.exp(cumul), jnp.exp(finals - cumul), finals


def set_cumuls(decay, cols_ref, rows_ref):
    triangle = lower_triangle().astype(F32).astype(BF16)
    cumul = dot(triangle, decay, 1, 1)
    rows = dot(decay, triangle, 1, 1)
    for step in range(2 * STEPS):
        heads = slice(step * PER_STEP, (step + 1) * PER_STEP)
        cols_ref[step] = cumul[:, heads]
        rows_ref[step] = rows[heads]


def head_states(query, key, value, grad, fwd, bwd):
    scaled_key = (key.astype(F32) * bwd).astype(BF16)
    scaled_query = (query.astype(F32) * fwd).astype(BF16)
    return dot(scaled_key, value, 0, 0), dot(scaled_query, grad, 0, 0)


def write_states(spot, rows, fwd, bwd, finals, outs):
    cols = slice(spot * HEAD, (spot + 1) * HEAD)
    one = slice(spot, spot + 1)
    query, key, value, grad = (ref[:, cols] for ref in rows)
    kv, qd = head_states(query, key, value, grad, fwd[:, one], bwd[:, one])
    tail = pack_decay(finals[:, one])
    for out_ref in outs:
        out_ref[spot, 0:HEAD, :] = kv.astype(out_ref.dtype)
        out_ref[spot, HEAD : 2 * HEAD, :] = qd.astype(out_ref.dtype)
        out_ref[spot, 2 * HEAD :, :] = tail.astype(out_ref.dtype)


def sent_states(half_ref, decay_hbm, *refs):
    sources, out_ref, away, rows = refs[:4], refs[4], refs[5:9], refs[9:13]
    decay_ref, sems, away_sems, decay_sem = refs[13:]
    half = half_ref[0]

    def fetch(array, at):
        source = pl.multiple_of(half * WIDTH + at * LOAD, LOAD)
        return pltpu.make_async_copy(
            sources[array].at[:, pl.ds(source, LOAD)],
            rows[array].at[:, at * LOAD : (at + 1) * LOAD],
            sems.at[array, at],
        )

    def fetch_away(array):
        source = pl.multiple_of((1 - half) * WIDTH, WIDTH)
        return pltpu.make_async_copy(
            sources[array].at[:, pl.ds(source, WIDTH)], away[array], away_sems.at[array]
        )

    decay_copy = pltpu.make_async_copy(decay_hbm, decay_ref, decay_sem.at[0])
    decay_copy.start()
    for array in range(4):
        fetch(array, 0).start()
    decay_copy.wait()
    fwd, bwd, finals = column_scales(half_decay(decay_ref, half))
    for array in range(4):
        fetch(array, 1).start()
    for spot in range(HALF_HEADS):
        if spot % (HALF_HEADS // LOADS) == 0:
            for array in range(4):
                fetch(array, spot // (HALF_HEADS // LOADS)).wait()
        if spot == PER_STEP:
            for array in range(4):
                fetch_away(array).start()
        write_states(spot, rows, fwd, bwd, finals, (out_ref,))
    for array in range(4):
        fetch_away(array).wait()


def kept_states(half_ref, decay_ref, *refs):
    rows, outs = refs[:4], refs[4:]
    fwd, bwd, finals = column_scales(half_decay(decay_ref, half_ref[0]))
    for spot in range(HALF_HEADS):
        write_states(spot, rows, fwd, bwd, finals, outs)


def pair_states(half_ref, own_ref, other_ref, out_hbm, mine_ref, their_ref, pair_ref, sems):
    kept_from = pl.multiple_of(half_ref[0] * HEAD, HEAD)
    their_from = pl.multiple_of((1 - half_ref[0]) * HEAD, HEAD)
    first = half_ref[0] == 0
    chunk = 2 * HALF_HEADS // STEPS

    def send(step):
        spots = slice(step * chunk, (step + 1) * chunk)
        return pltpu.make_async_copy(pair_ref.at[spots], out_hbm.at[spots], sems.at[step])

    for head in range(HALF_HEADS):
        mine = unpack_decay(own_ref[head, 2 * HEAD :, :])
        theirs = unpack_decay(other_ref[head, 2 * HEAD :, :])
        decay_mine = jnp.exp(mine)
        decay_theirs = jnp.exp(theirs)
        unit = jnp.ones_like(mine)
        kv_scales = (jnp.where(first, decay_theirs, unit), jnp.where(first, unit, decay_mine))
        qd_scales = (jnp.where(first, unit, decay_theirs), jnp.where(first, decay_mine, unit))
        tail = pack_decay(mine + theirs)
        for part in range(2):
            piece = 2 * head + part
            for at, (scale_own, scale_other) in ((0, kv_scales), (1, qd_scales)):
                rows = slice(at * HEAD + part * PART, at * HEAD + (part + 1) * PART)
                joined = scale_own * own_ref[head, rows, :] + scale_other * other_ref[
                    head, rows, :
                ].astype(F32)
                pair_ref[piece, at * PART : (at + 1) * PART, :] = joined.astype(BF16)
            pair_ref[piece, 2 * PART :, :] = tail
        if (head + 1) % PER_STEP == 0:
            send(head // PER_STEP).start()
    for head in range(HALF_HEADS):
        mine_ref[head, 0:HEAD, :] = own_ref[head, pl.ds(kept_from, HEAD), :].astype(BF16)
        mine_ref[head, HEAD:, :] = own_ref[head, 2 * HEAD :, :].astype(BF16)
        their_ref[head, 0:HEAD, :] = other_ref[head, pl.ds(their_from, HEAD), :]
        their_ref[head, HEAD:, :] = other_ref[head, 2 * HEAD :, :]
    for step in range(STEPS):
        send(step).wait()


def group_total(index_ref, pieces_ref, *outs):
    count = pieces_ref.shape[0]
    place = index_ref[0]
    zero = jnp.zeros((PART, HEAD), F32)

    def hop(at, carry):
        state, trail, total = carry
        back = count - 1 - at
        decay = unpack_decay(pieces_ref[at, 2 * PART :, :])
        decay_back = unpack_decay(pieces_ref[back, 2 * PART :, :])
        state = jnp.exp(decay) * state + pieces_ref[at, 0:PART, :].astype(F32)
        trail = jnp.exp(decay_back) * trail + pieces_ref[back, PART : 2 * PART, :].astype(F32)
        return state, trail, total + decay

    state, trail, total = lax.fori_loop(
        0, count, hop, (zero, zero, jnp.zeros((1, HEAD), F32)), unroll=8
    )
    tail = jnp.broadcast_to(total, (TAIL, HEAD))
    for distance, ref in zip(DISTANCES, outs):
        ref[0:PART, :] = jnp.where(place + distance <= len(outs), state, trail)
        ref[PART:, :] = tail


def group_entries(index_ref, pieces_ref, two_ref, one_ref, three_ref, out_ref):
    count = pieces_ref.shape[0]
    place = index_ref[0]
    state = jnp.zeros((PART, HEAD), F32)
    trail = jnp.zeros((PART, HEAD), F32)
    for distance, ref in ((3, three_ref), (2, two_ref), (1, one_ref)):
        longer = jnp.exp(ref[PART : PART + 1, :]) * state + ref[0:PART, :]
        state = jnp.where(place >= distance, longer, state)
    for distance, ref in ((1, one_ref), (2, two_ref), (3, three_ref)):
        longer = jnp.exp(ref[PART : PART + 1, :]) * trail + ref[0:PART, :]
        trail = jnp.where(place < distance, longer, trail)

    def hop(at, carry):
        state, trail = carry
        back = count - 1 - at
        out_ref[at, 0:PART, :] = state.astype(BF16)
        out_ref[back, PART : 2 * PART, :] = trail.astype(BF16)
        decay = unpack_decay(pieces_ref[at, 2 * PART :, :])
        decay_back = unpack_decay(pieces_ref[back, 2 * PART :, :])
        state = jnp.exp(decay) * state + pieces_ref[at, 0:PART, :].astype(F32)
        trail = jnp.exp(decay_back) * trail + pieces_ref[back, PART : 2 * PART, :].astype(F32)
        return state, trail

    lax.fori_loop(0, count, hop, (state, trail), unroll=8)


def write_entries(changed, states_ref, pair_ref, out_ref):
    step_from = pl.multiple_of(changed * PART, PART)
    same_from = pl.multiple_of((1 - changed) * PART, PART)
    for head in range(HALF_HEADS):
        decay = jnp.exp(unpack_decay(states_ref[head, HEAD:, :]))
        for part in range(2):
            lines = slice(part * PART, (part + 1) * PART)
            carried = pair_ref[2 * head + part, pl.ds(step_from, PART), :].astype(F32)
            joined = decay * carried + states_ref[head, lines, :].astype(F32)
            step_to = pl.multiple_of(changed * HEAD + part * PART, PART)
            same_to = pl.multiple_of((1 - changed) * HEAD + part * PART, PART)
            out_ref[head, pl.ds(step_to, PART), :] = joined.astype(BF16)
            out_ref[head, pl.ds(same_to, PART), :] = pair_ref[2 * head + part, pl.ds(same_from, PART), :]


def other_entries(half_ref, mine_ref, pair_ref, *refs):
    count = 8 - HELD
    held, out_ref, early, sems = refs[:count], refs[count], refs[count + 1 : -1], refs[-1]
    cols = pl.ds(pl.multiple_of(half_ref[0] * WIDTH, WIDTH), LOAD)
    copies = [
        pltpu.make_async_copy(held[at].at[:, cols], early[at], sems.at[at]) for at in range(count)
    ]
    for copy in copies:
        copy.start()
    write_entries(half_ref[0], mine_ref, pair_ref, out_ref)
    for copy in copies:
        copy.wait()


def inner_results(
    decay_ref, query_ref, key_ref, value_ref, grad_ref, att_ref, qg_ref, kg_ref, vg_ref, cols_ref, rows_ref
):
    step = pl.program_id(0)

    @pl.when(step == 0)
    def _():
        set_cumuls(decay_ref[...], cols_ref, rows_ref)

    lower = lower_triangle()
    for head in range(PER_STEP):
        cols = slice(head * HEAD, (head + 1) * HEAD)
        one = slice(head, head + 1)
        query, key, value, grad = (
            ref[:, cols] for ref in (query_ref, key_ref, value_ref, grad_ref)
        )
        spread = cols_ref[step][:, one] - rows_ref[step][one]
        weights = jnp.exp(jnp.where(lower, spread, -jnp.inf))
        probs = (dot(query, key, 1, 1) * weights).astype(BF16)
        grows = (dot(grad, value, 1, 1) * weights).astype(BF16)
        att_ref[:, cols] = dot(probs, value, 1, 0).astype(BF16)
        qg_ref[:, cols] = dot(grows, key, 1, 0).astype(BF16)
        kg_ref[:, cols] = dot(grows, query, 0, 0).astype(BF16)
        vg_ref[:, cols] = dot(probs, grad, 0, 0).astype(BF16)


def add_states(rows, inner, outs, spot, at, fwd, bwd, entering, trailing):
    cols = slice(spot * HEAD, (spot + 1) * HEAD)
    query, key, value, grad = (ref[:, cols] for ref in rows)
    terms = (
        fwd * dot(query, entering, 1, 0),
        fwd * dot(grad, entering, 1, 1),
        bwd * dot(value, trailing, 1, 1),
        bwd * dot(key, trailing, 1, 0),
    )
    for out, ref, term in zip(outs, inner, terms):
        out[:, at] = (ref[:, cols].astype(F32) + term).astype(BF16)


def result_copies(half, outs_hbm, outs, sems):
    def store(array, step):
        target = pl.multiple_of(half * WIDTH + step * SLAB, SLAB)
        return pltpu.make_async_copy(
            outs[array].at[:, step * SLAB : (step + 1) * SLAB],
            outs_hbm[array].at[:, pl.ds(target, SLAB)],
            sems.at[array, step],
        )

    return store


def own_results(half_ref, decay_ref, *refs):
    held, refs = refs[:8], refs[8:]
    kept, early, refs = refs[:HELD], refs[HELD:8], refs[8:]
    (pair_ref, their_ref), refs = refs[:2], refs[2:]
    outs, refs = refs[:4], refs[4:]
    away, refs = refs[:8], refs[8:]
    late, refs = refs[: 8 - HELD], refs[8 - HELD :]
    entry_ref, near_sems, away_sems = refs
    half = half_ref[0]

    def fetch(array):
        source = pl.multiple_of(half * WIDTH + LOAD, LOAD)
        return pltpu.make_async_copy(
            held[array].at[:, pl.ds(source, LOAD)], late[array - HELD], near_sems.at[array]
        )

    def fetch_away(array):
        source = pl.multiple_of((1 - half) * WIDTH, WIDTH)
        return pltpu.make_async_copy(
            held[array].at[:, pl.ds(source, WIDTH)], away[array], away_sems.at[array]
        )

    for array in range(HELD, 8):
        fetch(array).start()
    fwd, bwd, _ = column_scales(half_decay(decay_ref, half))
    write_entries(1 - half, their_ref, pair_ref, entry_ref)
    for array in range(8):
        fetch_away(array).start()
    for spot in range(HALF_HEADS):
        if spot == LOAD // HEAD:
            for array in range(HELD, 8):
                fetch(array).wait()
        rows = [ref.at[:, : LOAD] for ref in kept] + list(early)
        if spot >= LOAD // HEAD:
            rows = [ref.at[:, LOAD:] for ref in kept] + list(late)
        from_at = spot * HEAD % LOAD
        one = slice(spot, spot + 1)
        entry = entry_ref[spot]
        add_states(
            rows[:4], rows[4:], outs, from_at // HEAD, slice(spot * HEAD, (spot + 1) * HEAD),
            fwd[:, one], bwd[:, one], entry[0:HEAD], entry[HEAD:],
        )
    for array in range(8):
        fetch_away(array).wait()


def other_results(half_ref, decay_ref, *refs):
    away, entry_ref, ready = refs[:8], refs[8], refs[9:13]
    outs_hbm, outs, (out_sems, ready_sems) = refs[13:17], refs[17:21], refs[21:]
    half = half_ref[0]
    store = result_copies(half, outs_hbm, outs, out_sems)

    def store_ready(array):
        target = pl.multiple_of((1 - half) * WIDTH, WIDTH)
        return pltpu.make_async_copy(
            ready[array], outs_hbm[array].at[:, pl.ds(target, WIDTH)], ready_sems.at[array]
        )

    for array in range(4):
        store_ready(array).start()
    fwd, bwd, _ = column_scales(half_decay(decay_ref, half))
    for spot in range(HALF_HEADS):
        step, head = divmod(spot, PER_STEP)
        one = slice(spot, spot + 1)
        entry = entry_ref[spot]
        add_states(
            away[:4], away[4:], outs, spot, slice(spot * HEAD, (spot + 1) * HEAD),
            fwd[:, one], bwd[:, one], entry[0:HEAD], entry[HEAD:],
        )
        if head == PER_STEP - 1:
            for array in range(4):
                store(array, step).start()
    for array in range(4):
        store_ready(array).wait()
    for step in range(STEPS):
        for array in range(4):
            store(array, step).wait()


IN_VMEM = pl.BlockSpec(memory_space=pltpu.VMEM)
IN_HBM = pl.BlockSpec(memory_space=pl.ANY)
IN_SMEM = pl.BlockSpec(memory_space=pltpu.SMEM)
CUMULS = (
    pltpu.VMEM((2 * STEPS, BLOCK, PER_STEP), F32),
    pltpu.VMEM((2 * STEPS, PER_STEP, BLOCK), F32),
)


def once(kernel, operands, outputs, scratch=(), specs=None, out_specs=None, aliases=None):
    if specs is None:
        specs = [IN_SMEM if item.shape == (1,) else IN_VMEM for item in operands]
    return pl.pallas_call(
        kernel,
        out_shape=outputs,
        in_specs=specs,
        out_specs=out_specs or jax.tree.map(lambda _: IN_VMEM, outputs),
        scratch_shapes=list(scratch),
        input_output_aliases=aliases or {},
        compiler_params=pltpu.CompilerParams(vmem_limit_bytes=VMEM_LIMIT),
    )(*operands)


def in_hbm(item):
    return pltpu.with_memory_space_constraint(item, pltpu.HBM)


def shards(queries, key_rows, value_rows, out_grad, log_decay):
    core = lax.axis_index("core")
    mine = core.reshape(1).astype(jnp.int32)
    theirs = 1 - mine
    place = lax.axis_index("zh").reshape(1).astype(jnp.int32)
    rows = tuple(in_hbm(item) for item in (queries, key_rows, value_rows, out_grad))
    decay = log_decay.T
    decay_hbm = in_hbm(decay)
    state_rows = 2 * HEAD + TAIL
    piece_rows = 2 * PART + TAIL
    swap = [(0, 1), (1, 0)]
    states = (HALF_HEADS, state_rows, HEAD)
    pieces_shape = (2 * HALF_HEADS, piece_rows, HEAD)

    buffers = (pltpu.VMEM((BLOCK, WIDTH), BF16),)
    sent, *kept_rows = once(
        sent_states, (theirs, decay_hbm) + rows, [pltpu.VMEM(states, BF16)] + list(buffers * 4),
        buffers * 4
        + (
            pltpu.VMEM(decay.shape, BF16),
            pltpu.SemaphoreType.DMA((4, LOADS)),
            pltpu.SemaphoreType.DMA((4,)),
            pltpu.SemaphoreType.DMA((1,)),
        ),
        [IN_SMEM] + [IN_HBM] * 5,
    )
    other = lax.ppermute(sent, "core", swap)
    (own,) = once(kept_states, (mine, decay, *kept_rows), [pltpu.VMEM(states, F32)])
    part_states = pltpu.VMEM((HALF_HEADS, HEAD + TAIL, HEAD), BF16)
    pairs, own_part, other_part = once(
        pair_states, (mine, own, other), [pltpu.HBM(pieces_shape, BF16), part_states, part_states],
        (pltpu.VMEM(pieces_shape, BF16), pltpu.SemaphoreType.DMA((STEPS,))),
        out_specs=[IN_HBM, IN_VMEM, IN_VMEM],
    )
    pieces = lax.all_to_all(pairs, GROUP, split_axis=0, concat_axis=0, tiled=True)
    decay_later = lax.optimization_barrier((decay, pairs))[0]
    slab = pl.BlockSpec((BLOCK, SLAB), lambda step: (0, step))
    inner = pl.pallas_call(
        inner_results,
        out_shape=[pltpu.HBM(queries.shape, BF16)] * 4,
        grid_spec=pltpu.PrefetchScalarGridSpec(
            num_scalar_prefetch=0, grid=(2 * STEPS,),
            in_specs=[pl.BlockSpec(decay.shape, lambda step: (0, 0))] + [slab] * 4,
            out_specs=[slab] * 4, scratch_shapes=list(CUMULS),
        ),
        compiler_params=pltpu.CompilerParams(vmem_limit_bytes=VMEM_LIMIT),
    )(decay_later, *rows)
    pieces, inner = lax.optimization_barrier((pieces, inner))
    inner = tuple(in_hbm(item) for item in inner)
    size = lax.axis_size("zh")
    totals = once(group_total, (place, pieces), [pltpu.VMEM((PART + TAIL, HEAD), F32)] * (size - 1))
    moved = [
        lax.ppermute(total, "zh", [(at, (at + distance) % size) for at in range(size)])
        for distance, total in zip(DISTANCES, totals)
    ]
    entries = once(
        group_entries, (place, pieces, *moved), pltpu.VMEM((2 * HALF_HEADS, 2 * PART, HEAD), BF16)
    )
    pair_entries = lax.all_to_all(entries, GROUP, split_axis=0, concat_axis=0, tiled=True)
    short = (pltpu.VMEM((BLOCK, LOAD), BF16),) * (8 - HELD)
    leaving, *early = once(
        other_entries, (mine, own_part, pair_entries) + (rows + inner)[HELD:],
        [pltpu.VMEM((HALF_HEADS, 2 * HEAD, HEAD), BF16)] + list(short),
        (pltpu.SemaphoreType.DMA((8 - HELD,)),),
        [IN_SMEM] + [IN_VMEM] * 2 + [IN_HBM] * (8 - HELD),
    )
    arrived = lax.ppermute(leaving, "core", swap)
    results = once(
        own_results,
        (mine, decay) + rows + inner + tuple(kept_rows[:HELD]) + tuple(early) + (pair_entries, other_part),
        list(buffers * 12),
        short
        + (
            pltpu.VMEM((HALF_HEADS, 2 * HEAD, HEAD), BF16),
            pltpu.SemaphoreType.DMA((8,)),
            pltpu.SemaphoreType.DMA((8,)),
        ),
        [IN_SMEM, IN_VMEM] + [IN_HBM] * 8 + [IN_VMEM] * 10,
    )
    results = once(
        other_results, (theirs, decay) + tuple(results[4:]) + (arrived,) + tuple(results[:4]),
        [pltpu.HBM(queries.shape, BF16)] * 4,
        buffers * 4 + (pltpu.SemaphoreType.DMA((4, STEPS)), pltpu.SemaphoreType.DMA((4,))),
        out_specs=[IN_HBM] * 4,
    )
    return tuple(results)


def solution(mesh):
    chain, inner = mesh.devices.shape
    grid = Mesh(mesh.devices.reshape(chain // 2, 2, 4, 4, inner // 16), AXES)
    spec = P(AXES, None)
    return jax.shard_map(
        shards, mesh=grid, in_specs=(spec,) * 5, out_specs=(spec,) * 4, check_vma=False
    )
```

```python
import jax
import jax.numpy as jnp
from jax import lax
from jax.experimental import pallas as pl
from jax.experimental.pallas import tpu as pltpu
from jax.sharding import Mesh, PartitionSpec as P

HEAD = 128
BLOCK = 128
HALF_HEADS = 16
STEPS = 4
PER_STEP = HALF_HEADS // STEPS
PART = HEAD // 2
TAIL = 8
SLAB = PER_STEP * HEAD
WIDTH = HALF_HEADS * HEAD
LOADS = 2
LOAD = WIDTH // LOADS
HELD = 2
DISTANCES = (2, 1, 3)
AXES = ("zh", "zl", "y", "x", "core")
GROUP = ("zl", "y", "x")

F32 = jnp.float32
BF16 = jnp.bfloat16
VMEM_LIMIT = 16 * 1024 * 1024


def dot(left, right, left_dim, right_dim):
    return lax.dot_general(
        left, right, (((left_dim,), (right_dim,)), ((), ())), preferred_element_type=F32
    )


def pack_decay(value):
    full = jnp.broadcast_to(value, (TAIL, HEAD))
    high = full.astype(BF16)
    rest = full - high.astype(F32)
    middle = rest.astype(BF16)
    low = (rest - middle.astype(F32)).astype(BF16)
    row = lax.broadcasted_iota(jnp.int32, (TAIL, HEAD), 0)
    chosen = jnp.where(
        row == 0, high.astype(F32), jnp.where(row == 1, middle.astype(F32), low.astype(F32))
    )
    return chosen.astype(BF16)


def unpack_decay(tile):
    rows = tile.astype(F32)
    return rows[0:1] + rows[1:2] + rows[2:3]


def lower_triangle():
    at = lax.broadcasted_iota(jnp.int32, (BLOCK, BLOCK), 0)
    before = lax.broadcasted_iota(jnp.int32, (BLOCK, BLOCK), 1)
    return at >= before


def half_decay(decay_ref, half):
    decay = decay_ref[...].astype(F32)
    return jnp.where(half == 0, decay[:HALF_HEADS], decay[HALF_HEADS:]).astype(BF16)


def column_scales(decay):
    cumul = dot(lower_triangle().astype(F32).astype(BF16), decay, 1, 1)
    finals = cumul[BLOCK - 1 : BLOCK, :]
    return jnp.exp(cumul), jnp.exp(finals - cumul), finals


def set_cumuls(decay, cols_ref, rows_ref):
    triangle = lower_triangle().astype(F32).astype(BF16)
    cumul = dot(triangle, decay, 1, 1)
    rows = dot(decay, triangle, 1, 1)
    for step in range(2 * STEPS):
        heads = slice(step * PER_STEP, (step + 1) * PER_STEP)
        cols_ref[step] = cumul[:, heads]
        rows_ref[step] = rows[heads]


def head_states(query, key, value, grad, fwd, bwd):
    scaled_key = (key.astype(F32) * bwd).astype(BF16)
    scaled_query = (query.astype(F32) * fwd).astype(BF16)
    return dot(scaled_key, value, 0, 0), dot(scaled_query, grad, 0, 0)


def write_states(spot, rows, fwd, bwd, finals, outs):
    cols = slice(spot * HEAD, (spot + 1) * HEAD)
    one = slice(spot, spot + 1)
    query, key, value, grad = (ref[:, cols] for ref in rows)
    kv, qd = head_states(query, key, value, grad, fwd[:, one], bwd[:, one])
    tail = pack_decay(finals[:, one])
    for out_ref in outs:
        out_ref[spot, 0:HEAD, :] = kv.astype(out_ref.dtype)
        out_ref[spot, HEAD : 2 * HEAD, :] = qd.astype(out_ref.dtype)
        out_ref[spot, 2 * HEAD :, :] = tail.astype(out_ref.dtype)


def sent_states(half_ref, decay_hbm, *refs):
    sources, out_ref, away, rows = refs[:4], refs[4], refs[5:9], refs[9:13]
    decay_ref, sems, away_sems, decay_sem = refs[13:]
    half = half_ref[0]

    def fetch(array, at):
        source = pl.multiple_of(half * WIDTH + at * LOAD, LOAD)
        return pltpu.make_async_copy(
            sources[array].at[:, pl.ds(source, LOAD)],
            rows[array].at[:, at * LOAD : (at + 1) * LOAD],
            sems.at[array, at],
        )

    def fetch_away(array):
        source = pl.multiple_of((1 - half) * WIDTH, WIDTH)
        return pltpu.make_async_copy(
            sources[array].at[:, pl.ds(source, WIDTH)], away[array], away_sems.at[array]
        )

    decay_copy = pltpu.make_async_copy(decay_hbm, decay_ref, decay_sem.at[0])
    decay_copy.start()
    for array in range(4):
        fetch(array, 0).start()
    decay_copy.wait()
    fwd, bwd, finals = column_scales(half_decay(decay_ref, half))
    for array in range(4):
        fetch(array, 1).start()
    for spot in range(HALF_HEADS):
        if spot % (HALF_HEADS // LOADS) == 0:
            for array in range(4):
                fetch(array, spot // (HALF_HEADS // LOADS)).wait()
        if spot == PER_STEP:
            for array in range(4):
                fetch_away(array).start()
        write_states(spot, rows, fwd, bwd, finals, (out_ref,))
    for array in range(4):
        fetch_away(array).wait()


def kept_states(half_ref, decay_ref, *refs):
    rows, outs = refs[:4], refs[4:]
    fwd, bwd, finals = column_scales(half_decay(decay_ref, half_ref[0]))
    for spot in range(HALF_HEADS):
        write_states(spot, rows, fwd, bwd, finals, outs)


def pair_states(half_ref, own_ref, other_ref, out_hbm, mine_ref, their_ref, pair_ref, sems):
    kept_from = pl.multiple_of(half_ref[0] * HEAD, HEAD)
    their_from = pl.multiple_of((1 - half_ref[0]) * HEAD, HEAD)
    first = half_ref[0] == 0
    chunk = 2 * HALF_HEADS // STEPS

    def send(step):
        spots = slice(step * chunk, (step + 1) * chunk)
        return pltpu.make_async_copy(pair_ref.at[spots], out_hbm.at[spots], sems.at[step])

    for head in range(HALF_HEADS):
        mine = unpack_decay(own_ref[head, 2 * HEAD :, :])
        theirs = unpack_decay(other_ref[head, 2 * HEAD :, :])
        decay_mine = jnp.exp(mine)
        decay_theirs = jnp.exp(theirs)
        unit = jnp.ones_like(mine)
        kv_scales = (jnp.where(first, decay_theirs, unit), jnp.where(first, unit, decay_mine))
        qd_scales = (jnp.where(first, unit, decay_theirs), jnp.where(first, decay_mine, unit))
        tail = pack_decay(mine + theirs)
        for part in range(2):
            piece = 2 * head + part
            for at, (scale_own, scale_other) in ((0, kv_scales), (1, qd_scales)):
                rows = slice(at * HEAD + part * PART, at * HEAD + (part + 1) * PART)
                joined = scale_own * own_ref[head, rows, :] + scale_other * other_ref[
                    head, rows, :
                ].astype(F32)
                pair_ref[piece, at * PART : (at + 1) * PART, :] = joined.astype(BF16)
            pair_ref[piece, 2 * PART :, :] = tail
        if (head + 1) % PER_STEP == 0:
            send(head // PER_STEP).start()
    for head in range(HALF_HEADS):
        mine_ref[head, 0:HEAD, :] = own_ref[head, pl.ds(kept_from, HEAD), :].astype(BF16)
        mine_ref[head, HEAD:, :] = own_ref[head, 2 * HEAD :, :].astype(BF16)
        their_ref[head, 0:HEAD, :] = other_ref[head, pl.ds(their_from, HEAD), :]
        their_ref[head, HEAD:, :] = other_ref[head, 2 * HEAD :, :]
    for step in range(STEPS):
        send(step).wait()


def group_total(index_ref, pieces_ref, *outs):
    count = pieces_ref.shape[0]
    place = index_ref[0]
    zero = jnp.zeros((PART, HEAD), F32)

    def hop(at, carry):
        state, trail, total = carry
        back = count - 1 - at
        decay = unpack_decay(pieces_ref[at, 2 * PART :, :])
        decay_back = unpack_decay(pieces_ref[back, 2 * PART :, :])
        state = jnp.exp(decay) * state + pieces_ref[at, 0:PART, :].astype(F32)
        trail = jnp.exp(decay_back) * trail + pieces_ref[back, PART : 2 * PART, :].astype(F32)
        return state, trail, total + decay

    state, trail, total = lax.fori_loop(
        0, count, hop, (zero, zero, jnp.zeros((1, HEAD), F32)), unroll=8
    )
    tail = pack_decay(total)
    for distance, ref in zip(DISTANCES, outs):
        ref[0:PART, :] = jnp.where(place + distance <= len(outs), state, trail).astype(BF16)
        ref[PART:, :] = tail


def group_entries(index_ref, pieces_ref, two_ref, one_ref, three_ref, out_ref):
    count = pieces_ref.shape[0]
    place = index_ref[0]
    state = jnp.zeros((PART, HEAD), F32)
    trail = jnp.zeros((PART, HEAD), F32)
    for distance, ref in ((3, three_ref), (2, two_ref), (1, one_ref)):
        longer = jnp.exp(unpack_decay(ref[PART:, :])) * state + ref[0:PART, :].astype(F32)
        state = jnp.where(place >= distance, longer, state)
    for distance, ref in ((1, one_ref), (2, two_ref), (3, three_ref)):
        longer = jnp.exp(unpack_decay(ref[PART:, :])) * trail + ref[0:PART, :].astype(F32)
        trail = jnp.where(place < distance, longer, trail)

    def hop(at, carry):
        state, trail = carry
        back = count - 1 - at
        out_ref[at, 0:PART, :] = state.astype(BF16)
        out_ref[back, PART : 2 * PART, :] = trail.astype(BF16)
        decay = unpack_decay(pieces_ref[at, 2 * PART :, :])
        decay_back = unpack_decay(pieces_ref[back, 2 * PART :, :])
        state = jnp.exp(decay) * state + pieces_ref[at, 0:PART, :].astype(F32)
        trail = jnp.exp(decay_back) * trail + pieces_ref[back, PART : 2 * PART, :].astype(F32)
        return state, trail

    lax.fori_loop(0, count, hop, (state, trail), unroll=8)


def write_entries(changed, states_ref, pair_ref, out_ref):
    step_from = pl.multiple_of(changed * PART, PART)
    same_from = pl.multiple_of((1 - changed) * PART, PART)
    for head in range(HALF_HEADS):
        decay = jnp.exp(unpack_decay(states_ref[head, HEAD:, :]))
        for part in range(2):
            lines = slice(part * PART, (part + 1) * PART)
            carried = pair_ref[2 * head + part, pl.ds(step_from, PART), :].astype(F32)
            joined = decay * carried + states_ref[head, lines, :].astype(F32)
            step_to = pl.multiple_of(changed * HEAD + part * PART, PART)
            same_to = pl.multiple_of((1 - changed) * HEAD + part * PART, PART)
            out_ref[head, pl.ds(step_to, PART), :] = joined.astype(BF16)
            out_ref[head, pl.ds(same_to, PART), :] = pair_ref[2 * head + part, pl.ds(same_from, PART), :]


def other_entries(half_ref, mine_ref, pair_ref, out_ref):
    write_entries(half_ref[0], mine_ref, pair_ref, out_ref)


def inner_results(
    decay_ref, query_ref, key_ref, value_ref, grad_ref, att_ref, qg_ref, kg_ref, vg_ref, cols_ref, rows_ref
):
    step = pl.program_id(0)

    @pl.when(step == 0)
    def _():
        set_cumuls(decay_ref[...], cols_ref, rows_ref)

    lower = lower_triangle()
    for head in range(PER_STEP):
        cols = slice(head * HEAD, (head + 1) * HEAD)
        one = slice(head, head + 1)
        query, key, value, grad = (
            ref[:, cols] for ref in (query_ref, key_ref, value_ref, grad_ref)
        )
        spread = cols_ref[step][:, one] - rows_ref[step][one]
        weights = jnp.exp(jnp.where(lower, spread, -jnp.inf))
        probs = (dot(query, key, 1, 1) * weights).astype(BF16)
        grows = (dot(grad, value, 1, 1) * weights).astype(BF16)
        att_ref[:, cols] = dot(probs, value, 1, 0).astype(BF16)
        qg_ref[:, cols] = dot(grows, key, 1, 0).astype(BF16)
        kg_ref[:, cols] = dot(grows, query, 0, 0).astype(BF16)
        vg_ref[:, cols] = dot(probs, grad, 0, 0).astype(BF16)


def add_states(rows, inner, outs, spot, at, fwd, bwd, entering, trailing):
    cols = slice(spot * HEAD, (spot + 1) * HEAD)
    query, key, value, grad = (ref[:, cols] for ref in rows)
    terms = (
        fwd * dot(query, entering, 1, 0),
        fwd * dot(grad, entering, 1, 1),
        bwd * dot(value, trailing, 1, 1),
        bwd * dot(key, trailing, 1, 0),
    )
    for out, ref, term in zip(outs, inner, terms):
        out[:, at] = (ref[:, cols].astype(F32) + term).astype(BF16)


def result_copies(half, outs_hbm, outs, sems):
    def store(array, step):
        target = pl.multiple_of(half * WIDTH + step * SLAB, SLAB)
        return pltpu.make_async_copy(
            outs[array].at[:, step * SLAB : (step + 1) * SLAB],
            outs_hbm[array].at[:, pl.ds(target, SLAB)],
            sems.at[array, step],
        )

    return store


def own_results(half_ref, decay_ref, *refs):
    held, refs = refs[:8], refs[8:]
    near, (pair_ref, their_ref), refs = refs[:HELD], refs[HELD : HELD + 2], refs[HELD + 2 :]
    outs, refs = refs[:4], refs[4:]
    away, refs = refs[:8], refs[8:]
    near, refs = near + refs[: 8 - HELD], refs[8 - HELD :]
    entry_ref, near_sems, away_sems = refs
    half = half_ref[0]

    def fetch(array, at):
        source = pl.multiple_of(half * WIDTH + at * LOAD, LOAD)
        return pltpu.make_async_copy(
            held[array].at[:, pl.ds(source, LOAD)],
            near[array].at[:, at * LOAD : (at + 1) * LOAD],
            near_sems.at[array, at],
        )

    def fetch_away(array):
        source = pl.multiple_of((1 - half) * WIDTH, WIDTH)
        return pltpu.make_async_copy(
            held[array].at[:, pl.ds(source, WIDTH)], away[array], away_sems.at[array]
        )

    for array in range(HELD, 8):
        fetch(array, 0).start()
    fwd, bwd, _ = column_scales(half_decay(decay_ref, half))
    write_entries(1 - half, their_ref, pair_ref, entry_ref)
    for array in range(HELD, 8):
        fetch(array, 1).start()
    for spot in range(HALF_HEADS):
        if spot % (HALF_HEADS // LOADS) == 0:
            for array in range(HELD, 8):
                fetch(array, spot // (HALF_HEADS // LOADS)).wait()
        if spot == PER_STEP:
            for array in range(8):
                fetch_away(array).start()
        one = slice(spot, spot + 1)
        entry = entry_ref[spot]
        add_states(
            near[:4], near[4:], outs, spot, slice(spot * HEAD, (spot + 1) * HEAD),
            fwd[:, one], bwd[:, one], entry[0:HEAD], entry[HEAD:],
        )
    for array in range(8):
        fetch_away(array).wait()


def other_results(half_ref, decay_ref, *refs):
    away, entry_ref, ready = refs[:8], refs[8], refs[9:13]
    outs_hbm, outs, (out_sems, ready_sems) = refs[13:17], refs[17:21], refs[21:]
    half = half_ref[0]
    store = result_copies(half, outs_hbm, outs, out_sems)

    def store_ready(array):
        target = pl.multiple_of((1 - half) * WIDTH, WIDTH)
        return pltpu.make_async_copy(
            ready[array], outs_hbm[array].at[:, pl.ds(target, WIDTH)], ready_sems.at[array]
        )

    for array in range(4):
        store_ready(array).start()
    fwd, bwd, _ = column_scales(half_decay(decay_ref, half))
    for spot in range(HALF_HEADS):
        step, head = divmod(spot, PER_STEP)
        one = slice(spot, spot + 1)
        entry = entry_ref[spot]
        add_states(
            away[:4], away[4:], outs, spot, slice(spot * HEAD, (spot + 1) * HEAD),
            fwd[:, one], bwd[:, one], entry[0:HEAD], entry[HEAD:],
        )
        if head == PER_STEP - 1:
            for array in range(4):
                store(array, step).start()
    for array in range(4):
        store_ready(array).wait()
    for step in range(STEPS):
        for array in range(4):
            store(array, step).wait()


IN_VMEM = pl.BlockSpec(memory_space=pltpu.VMEM)
IN_HBM = pl.BlockSpec(memory_space=pl.ANY)
IN_SMEM = pl.BlockSpec(memory_space=pltpu.SMEM)
CUMULS = (
    pltpu.VMEM((2 * STEPS, BLOCK, PER_STEP), F32),
    pltpu.VMEM((2 * STEPS, PER_STEP, BLOCK), F32),
)


def once(kernel, operands, outputs, scratch=(), specs=None, out_specs=None, aliases=None):
    if specs is None:
        specs = [IN_SMEM if item.shape == (1,) else IN_VMEM for item in operands]
    return pl.pallas_call(
        kernel,
        out_shape=outputs,
        in_specs=specs,
        out_specs=out_specs or jax.tree.map(lambda _: IN_VMEM, outputs),
        scratch_shapes=list(scratch),
        input_output_aliases=aliases or {},
        compiler_params=pltpu.CompilerParams(vmem_limit_bytes=VMEM_LIMIT),
    )(*operands)


def in_hbm(item):
    return pltpu.with_memory_space_constraint(item, pltpu.HBM)


def shards(queries, key_rows, value_rows, out_grad, log_decay):
    core = lax.axis_index("core")
    mine = core.reshape(1).astype(jnp.int32)
    theirs = 1 - mine
    place = lax.axis_index("zh").reshape(1).astype(jnp.int32)
    rows = tuple(in_hbm(item) for item in (queries, key_rows, value_rows, out_grad))
    decay = log_decay.T
    decay_hbm = in_hbm(decay)
    state_rows = 2 * HEAD + TAIL
    piece_rows = 2 * PART + TAIL
    swap = [(0, 1), (1, 0)]
    states = (HALF_HEADS, state_rows, HEAD)
    pieces_shape = (2 * HALF_HEADS, piece_rows, HEAD)

    buffers = (pltpu.VMEM((BLOCK, WIDTH), BF16),)
    sent, *kept_rows = once(
        sent_states, (theirs, decay_hbm) + rows, [pltpu.VMEM(states, BF16)] + list(buffers * 4),
        buffers * 4
        + (
            pltpu.VMEM(decay.shape, BF16),
            pltpu.SemaphoreType.DMA((4, LOADS)),
            pltpu.SemaphoreType.DMA((4,)),
            pltpu.SemaphoreType.DMA((1,)),
        ),
        [IN_SMEM] + [IN_HBM] * 5,
    )
    other = lax.ppermute(sent, "core", swap)
    (own,) = once(kept_states, (mine, decay, *kept_rows), [pltpu.VMEM(states, F32)])
    part_states = pltpu.VMEM((HALF_HEADS, HEAD + TAIL, HEAD), BF16)
    pairs, own_part, other_part = once(
        pair_states, (mine, own, other), [pltpu.HBM(pieces_shape, BF16), part_states, part_states],
        (pltpu.VMEM(pieces_shape, BF16), pltpu.SemaphoreType.DMA((STEPS,))),
        out_specs=[IN_HBM, IN_VMEM, IN_VMEM],
    )
    pieces = lax.all_to_all(pairs, GROUP, split_axis=0, concat_axis=0, tiled=True)
    decay_later = lax.optimization_barrier((decay, pairs))[0]
    slab = pl.BlockSpec((BLOCK, SLAB), lambda step: (0, step))
    inner = pl.pallas_call(
        inner_results,
        out_shape=[pltpu.HBM(queries.shape, BF16)] * 4,
        grid_spec=pltpu.PrefetchScalarGridSpec(
            num_scalar_prefetch=0, grid=(2 * STEPS,),
            in_specs=[pl.BlockSpec(decay.shape, lambda step: (0, 0))] + [slab] * 4,
            out_specs=[slab] * 4, scratch_shapes=list(CUMULS),
        ),
        compiler_params=pltpu.CompilerParams(vmem_limit_bytes=VMEM_LIMIT),
    )(decay_later, *rows)
    pieces, inner = lax.optimization_barrier((pieces, inner))
    inner = tuple(in_hbm(item) for item in inner)
    size = lax.axis_size("zh")
    totals = once(group_total, (place, pieces), [pltpu.VMEM((PART + TAIL, HEAD), BF16)] * (size - 1))
    moved = [
        lax.ppermute(total, "zh", [(at, (at + distance) % size) for at in range(size)])
        for distance, total in zip(DISTANCES, totals)
    ]
    entries = once(
        group_entries, (place, pieces, *moved), pltpu.VMEM((2 * HALF_HEADS, 2 * PART, HEAD), BF16)
    )
    pair_entries = lax.all_to_all(entries, GROUP, split_axis=0, concat_axis=0, tiled=True)
    leaving = once(
        other_entries, (mine, own_part, pair_entries), pltpu.VMEM((HALF_HEADS, 2 * HEAD, HEAD), BF16)
    )
    arrived = lax.ppermute(leaving, "core", swap)
    results = once(
        own_results, (mine, decay) + rows + inner + tuple(kept_rows[:HELD]) + (pair_entries, other_part),
        list(buffers * 12),
        buffers * (8 - HELD)
        + (
            pltpu.VMEM((HALF_HEADS, 2 * HEAD, HEAD), BF16),
            pltpu.SemaphoreType.DMA((8, LOADS)),
            pltpu.SemaphoreType.DMA((8,)),
        ),
        [IN_SMEM, IN_VMEM] + [IN_HBM] * 8 + [IN_VMEM] * (2 + HELD),
    )
    results = once(
        other_results, (theirs, decay) + tuple(results[4:]) + (arrived,) + tuple(results[:4]),
        [pltpu.HBM(queries.shape, BF16)] * 4,
        buffers * 4 + (pltpu.SemaphoreType.DMA((4, STEPS)), pltpu.SemaphoreType.DMA((4,))),
        out_specs=[IN_HBM] * 4,
    )
    return tuple(results)


def solution(mesh):
    chain, inner = mesh.devices.shape
    grid = Mesh(mesh.devices.reshape(chain // 2, 2, 4, 4, inner // 16), AXES)
    spec = P(AXES, None)
    return jax.shard_map(
        shards, mesh=grid, in_specs=(spec,) * 5, out_specs=(spec,) * 4, check_vma=False
    )
```
